32 devices in a mesh: groups: 2 (over y), tile: 4 (over z), sub: 2 (over x), rep: 2 (over core).
Axes of the slice: x: 2, y: 2, z: 4, core: 2. Of those that a mesh axis runs over, the one named last changes fastest.
Arguments:
- pressure: float32 [64, 32, 256], P(('groups', 'tile'), 'sub', 'rep'), parts along dimension 0, may hold values from -3 to 3
- previous_pressure: float32 [64, 32, 256], P(('groups', 'tile'), 'sub', 'rep'), parts along dimension 0, may hold values from -3 to 3
- courant_square: float32 [64, 32, 256], P(('groups', 'tile'), 'sub', 'rep'), parts along dimension 0, may hold values from 0.07 to 0.22
- node_area: float32 [12288], P(('groups', 'tile', 'sub', 'rep')), parts along dimension 0, may hold values from 0.25 to 4
- mode_shapes: bfloat16 [12288, 2048], P(('groups', 'tile', 'sub', 'rep')), parts along dimension 0, may hold values from -0.049804688 to 0.049804688
- frequency: float32 [4096], P('groups'), parts along dimension 0, may hold values from 0.4 to 1.3
- damping_ratio: float32 [4096], P('groups'), parts along dimension 0, may hold values from 0.02 to 0.4
- modal_start: float32 [2, 4096], P(None, 'groups'), parts along dimension 1, may hold values from -4 to 4
- slot_cell: int32 [8, 2, 2, 384], P(('groups', 'tile'), 'sub', 'rep'), parts along dimension 0, may hold values from 0 to 16383, as said below
- slot_owner: int32 [8, 2, 2, 384, 1], P(('groups', 'tile'), 'sub', 'rep'), parts along dimension 0, may hold values from 0 to 3; in each aligned block of 384 rows (0 to 383, 384 to 767, ..., all dimensions but the last counted through in order) at most 96 rows name the same one
- surface_count: int32 [4, 2, 4], P(('groups', 'sub'), 'rep', 'tile'), parts along dimension 0, may hold values from 1 to 384, 512 in all within a row
Outputs:
- final_pressure: float32 [64, 32, 256], P(('groups', 'tile'), 'sub', 'rep'), parts along dimension 0
- prior_pressure: float32 [64, 32, 256], P(('groups', 'tile'), 'sub', 'rep'), parts along dimension 0
- surface_accel: bfloat16 [8, 2, 2, 4, 384], P(('groups', 'tile'), 'sub', 'rep'), parts along dimension 0
- modal_state: float32 [2, 4096], P(None, ('groups', 'tile', 'sub', 'rep')), parts along dimension 1
The draws below stay inside these ranges and needn't reach their ends.
There are 2 independent parts, one for each index of `groups`. The reference program is written for one: setup_inputs(seed, part) draws one part's arguments, and reference() takes and returns one part's arrays. A program takes and returns all parts, laid end to end along the dimension named above; each array names one. Nothing has to cross between parts.
Inputs may be any that keep to these rules, and one draw needn't show every extreme that they name: `slot_cell`: slot j of a block lies in the block's cells j * (42) to (j + 1) (42) - 1, so a block's slots name distinct cells. `slot_owner`: every owner index is named by exactly 96 of the 384 slots of each block (t, s, r). `surface_count`: for fixed s and r the counts over t sum to 128 times the number of tile indices, and one of them equals 384.
All inputs are finite; a program needn't handle non-finite values. No bound on the sum of `surface_count` on one device may be relied on, other than what follows from the above.
Results may differ from the reference program's by a relative error of at most 0.0098.
Values may be sent and summed in bfloat16 or wider, within the bound.
A program may use at most 64 MiB of HBM per device.

```python
import math
import jax
import jax.numpy as jnp
import numpy as np
from jax import lax

CX = 8
CY = 16
CZ = 128
STEPS = 4
SLOTS = 384
MODES = 2048
SURF_MEAN = 128
CAP = 96
CELLS = 16384
NX = 32
NY = 32
NZ = 256
NODES = 6144
N_TILE = 4
N_SUB = 2
N_REP = 2


def draw_slot_cell(key, part):
    stride = CELLS // SLOTS
    offset = jax.random.randint(key, (N_TILE, N_SUB, N_REP, SLOTS), 0, stride, dtype=jnp.int32)
    return jnp.arange(SLOTS, dtype=jnp.int32) * stride + offset


def spiked(result, key, source, target, shards_of, factor):
    def block_of(axis_at):
        return (jnp.arange(result.shape[axis_at]) // (result.shape[axis_at] // shards_of)).reshape((-1,) + (1,) * (result.ndim - 1 - axis_at))

    near = jax.random.permutation(key, shards_of)[block_of(target)]
    second = (block_of(target) + shards_of // 2) % shards_of
    return jnp.where((block_of(source) == near) | (block_of(source) == second), factor * result, result)


def level_of(stream_key, dims, shards, low, largest):
    level = 1.0
    for dim, shards_of in shards:
        heights = jax.random.uniform(jax.random.fold_in(jax.random.fold_in(stream_key, 6), dim), (shards_of,), jnp.float32, low / len(shards), largest / len(shards))
        level = level * jnp.repeat(jnp.exp(heights), dims[dim] // shards_of).reshape((-1,) + (1,) * (len(dims) - 1 - dim))
    return level


def length_profile(number_of, total, bound, slope):
    portions = [(1 << 20) // math.isqrt(standing ** slope) + 1 for standing in range(2, number_of + 1)]
    rest, holding = total - bound - (number_of - 1), [1] * (number_of - 1)
    while rest > 0:
        candidates = [i for i in range(number_of - 1) if holding[i] < bound]
        mass, budget = sum([portions[i] for i in candidates]), rest
        for i in candidates:
            more = min(bound - holding[i], max(1, budget * portions[i] // mass), rest)
            holding[i] = holding[i] + more
            rest = rest - more
    return np.array([bound] + holding)


def ragged_sizes(own_key, count, total, bound, lean):
    if count == 2:
        one = jax.random.randint(own_key, (), max(1, total - bound), min(bound, total - 1) + 1)
        return jnp.stack([one, total - one])
    sizes = jnp.asarray(length_profile(count, total, bound, lean), jnp.int32)
    couples = (count - 1) // 2
    giver, receiver = sizes[1:1 + 2 * couples:2], sizes[2:2 + 2 * couples:2]
    room = jnp.minimum(giver - 1, bound - receiver)
    passed = jax.random.randint(jax.random.fold_in(own_key, 1), (couples,), 0, 1 << 20) % (room + 1)
    sizes = sizes.at[1:1 + 2 * couples:2].set(giver - passed).at[2:2 + 2 * couples:2].set(receiver + passed)
    return sizes[jax.random.permutation(jax.random.fold_in(own_key, 2), count)]


def shared_out(key, own, number, rows, number_of, top, bound, skew):
    ranking = jax.random.permutation(key, number_of)
    heavy_load, ordinary = shares(number_of, rows * top, bound, skew, True), shares(number_of, rows * top, bound, skew, False)
    places = jnp.arange(number_of)

    def named(tallies, rotation):
        used = int((tallies > 0).sum())
        fixed = max(1, used // 4)
        passed = fixed + (places - fixed + rotation * (used - fixed)) % max(1, number_of - fixed)
        return jnp.zeros((number_of,), jnp.int32).at[ranking[jnp.where(places < fixed, places, passed)]].set(jnp.asarray(tallies, jnp.int32))

    tallies = jnp.where(number % 4 == 0, named(heavy_load, number // 4), named(ordinary, number - number // 4 - 1))
    mixed = jax.random.permutation(jax.random.fold_in(own, 3), number_of)
    donor, receiver = mixed[0:number_of // 2 * 2:2], mixed[1:number_of // 2 * 2:2]
    margin = jnp.minimum(tallies[donor] - 1, bound - tallies[receiver]) // 2
    margin = jnp.where((donor == ranking[0]) | (receiver == ranking[0]) | (tallies[receiver] == 0), 0, jnp.maximum(margin, 0))
    passed = jax.random.randint(jax.random.fold_in(own, 4), (number_of // 2,), 0, 1 << 20) % (margin + 1)
    tallies = tallies.at[donor].add(-passed).at[receiver].add(passed)
    members = jnp.searchsorted(jnp.cumsum(tallies), jnp.arange(rows * top), side="right").astype(jnp.int32)
    table = members.reshape(top, rows).T
    table = table[jax.random.permutation(jax.random.fold_in(own, 1), rows)]
    rotation = jax.random.randint(jax.random.fold_in(own, 2), (rows, 1), 0, top)
    return jnp.take_along_axis(table, (jnp.arange(top)[None, :] + rotation) % top, axis=1)


def shares(amount, total, bound, skew, full):
    portions = [(1 << 20) // math.isqrt(grade ** skew) + 1 for grade in range(1, amount + 1)]
    largest = bound if full else min(bound, max(-(-total // amount), total * portions[0] // sum(portions)))
    least = 1 if total - largest >= amount - 1 else 0
    holding, spare = [largest] + [least] * (amount - 1), total - largest - least * (amount - 1)
    while spare > 0:
        free = [i for i in range(1, amount) if holding[i] < largest] or [i for i in range(1, amount) if holding[i] < bound]
        pool, left = sum([portions[i] for i in free]), spare
        for i in free:
            more = min(bound - holding[i], max(1, left * portions[i] // pool), spare)
            holding[i] = holding[i] + more
            spare = spare - more
    return np.array(holding)


def scatter_about(stream_key, extent, width, limit, cuts=(), kind=jnp.bfloat16):
    loudness = level_of(stream_key, extent, cuts, -0.22, 0.18) if cuts else 1.0
    drawn = jax.random.normal(stream_key, extent, jnp.float32) * width * loudness
    return jnp.minimum(jnp.maximum(drawn, -limit), limit).astype(kind)


def gaussian_with(key, dims, deviation, reach, split, heavy, kind=jnp.bfloat16):
    entries = deviation * jax.random.normal(key, dims, jnp.float32)
    if split:
        entries = entries * level_of(key, dims, split, -0.22, 0.18)
    return jnp.clip(spiked(entries, jax.random.fold_in(key, 3), *heavy), -reach, reach).astype(kind)


def setup_inputs(seed: int = 0, part: int = 0) -> dict:
    splits = jax.random.split(jax.random.key(seed), 12)
    part_splits = jax.random.split(jax.random.fold_in(splits[11], part), 12)
    pressure = scatter_about(part_splits[0], (NX, NY, NZ), 0.5, 3.0, ((0, 4), (1, 2), (2, 2)), jnp.float32)
    previous_pressure = scatter_about(part_splits[1], (NX, NY, NZ), 0.5, 3.0, ((0, 4), (1, 2), (2, 2)), jnp.float32)
    courant_square = jnp.clip(0.07 + 0.15 * jax.random.uniform(part_splits[2], (NX, NY, NZ), jnp.float32) ** level_of(part_splits[2], (NX, NY, NZ), ((0, 4), (1, 2), (2, 2)), -0.2, 0.2), 0.07, 0.22)
    node_area = jnp.clip(jnp.exp(math.log(4.0) - 2.7725887 * jax.random.uniform(part_splits[3], (NODES,), jnp.float32) ** level_of(part_splits[3], (NODES,), ((0, 16),), -0.2, 0.2)), 0.25, 4.0)
    mode_shapes = gaussian_with(part_splits[4], (NODES, MODES), 0.008, 0.049804688, ((0, 16),), (0, 1, 16, 2.0))
    frequency = jnp.clip(jnp.exp(jax.random.uniform(part_splits[5], (MODES,), jnp.float32, math.log(0.4), math.log(1.3))), 0.4, 1.3)
    damping_ratio = jnp.clip(jnp.exp(jax.random.uniform(part_splits[6], (MODES,), jnp.float32, math.log(0.02), math.log(0.4))), 0.02, 0.4)
    modal_start = scatter_about(part_splits[7], (2, MODES), 1.0, 4.0, (), jnp.float32)
    slot_cell = draw_slot_cell(jax.random.fold_in(jax.random.fold_in(splits[11], part), 71), part)
    slot_owner_keys = jax.random.split(jax.random.fold_in(part_splits[9], 1), N_TILE * N_SUB * N_REP * SLOTS // SLOTS)
    slot_owner_turns = jax.random.permutation(jax.random.fold_in(part_splits[9], 3), N_TILE * N_SUB * N_REP * SLOTS // SLOTS)
    slot_owner = jax.vmap(lambda own, number: shared_out(jax.random.fold_in(part_splits[9], 2), own, number, SLOTS, N_TILE, 1, CAP, 0))(slot_owner_keys, slot_owner_turns).reshape((N_TILE, N_SUB, N_REP, SLOTS, 1))
    surface_count = jax.vmap(lambda own: ragged_sizes(own, N_TILE, N_TILE * SURF_MEAN, SLOTS, 2))(jax.random.split(part_splits[10], N_SUB * N_REP)).reshape((N_SUB, N_REP, N_TILE)).astype(jnp.int32)
    return dict(pressure=pressure, previous_pressure=previous_pressure, courant_square=courant_square, node_area=node_area, mode_shapes=mode_shapes, frequency=frequency, damping_ratio=damping_ratio, modal_start=modal_start, slot_cell=slot_cell, slot_owner=slot_owner, surface_count=surface_count)


nonlinear = 0.03
viscous = 0.02


def laplace(padded):
    middle = padded[1:-1, 1:-1, 1:-1]
    summed = padded[2:, 1:-1, 1:-1] + padded[:-2, 1:-1, 1:-1]
    summed = summed + padded[1:-1, 2:, 1:-1] + padded[1:-1, :-2, 1:-1]
    summed = summed + padded[1:-1, 1:-1, 2:] + padded[1:-1, 1:-1, :-2]
    return summed - 6.0 * middle


def advance(wide_now, wide_before, coefficient):
    current = wide_now[1:-1, 1:-1, 1:-1]
    before = wide_before[1:-1, 1:-1, 1:-1]
    change = current - before
    driving = coefficient * laplace(wide_now) + viscous * laplace(wide_now - wide_before) + 2.0 * nonlinear * change * change
    return 2.0 * current - before + (1.0 + 2.0 * nonlinear * current) * driving


def routing(owners, live_count, tile_total):
    slot_total = owners.shape[0]
    bucket = slot_total // tile_total
    position = jnp.arange(slot_total, dtype=jnp.int32)
    is_live = position < live_count
    member = ((owners[:, None] == jnp.arange(tile_total, dtype=jnp.int32)[None, :]) & is_live[:, None]).astype(jnp.float32)
    earlier = (position[None, :] < position[:, None]).astype(jnp.float32)
    before = jnp.dot(earlier, member, precision=lax.Precision.HIGHEST)
    bucket_rank = jnp.sum(before * member, axis=1).astype(jnp.int32)
    target = owners * bucket + bucket_rank
    return ((target[:, None] == position[None, :]) & is_live[:, None]).astype(jnp.bfloat16)


def oscillate(forces, frequency, damping_ratio, start_state):
    def advance_mode(carried, force_row):
        displace, velocity = carried
        acceleration = force_row - 2.0 * damping_ratio * frequency * velocity - frequency * frequency * displace
        velocity = velocity + acceleration
        displace = displace + velocity
        return (displace, velocity), acceleration

    (displace, velocity), modal_accel = lax.scan(advance_mode, (start_state[0], start_state[1]), forces)
    return modal_accel, jnp.stack([displace, velocity])


def reference(pressure, previous_pressure, courant_square, node_area, mode_shapes, frequency, damping_ratio, modal_start, slot_cell, slot_owner, surface_count):
    devices = N_TILE * N_SUB * N_REP
    bucket = SLOTS // N_TILE
    cell_first = slot_cell // (CY * CZ)
    cell_second = (slot_cell // CZ) % CY
    cell_third = slot_cell % CZ
    grid_first = jnp.arange(N_TILE, dtype=jnp.int32)[:, None, None, None] * CX + cell_first
    grid_second = jnp.arange(N_SUB, dtype=jnp.int32)[None, :, None, None] * CY + cell_second
    grid_third = jnp.arange(N_REP, dtype=jnp.int32)[None, None, :, None] * CZ + cell_third
    flat_index = ((grid_first * NY + grid_second) * NZ + grid_third).astype(jnp.int32)
    counts = jnp.transpose(surface_count, (2, 0, 1))
    is_live = jnp.arange(SLOTS, dtype=jnp.int32)[None, None, None, :] < counts[..., None]
    grid_now = pressure
    grid_before = previous_pressure
    records = []
    for step_index in range(STEPS):
        updated = advance(jnp.pad(grid_now, 1), jnp.pad(grid_before, 1), courant_square)
        records.append(jnp.take(updated.reshape(-1), flat_index))
        grid_before = grid_now
        grid_now = updated
    history = jnp.where(is_live[:, :, :, None, :], jnp.stack(records, axis=3), jnp.float32(0.0)).astype(jnp.bfloat16)

    def route_for(owners, live_count):
        return routing(owners, live_count, N_TILE)

    routes = jax.vmap(route_for)(slot_owner.reshape(devices, SLOTS), counts.reshape(devices))
    loads = jnp.einsum("dns,dst->dnt", history.reshape(devices, STEPS, SLOTS).astype(jnp.float32), routes.astype(jnp.float32))
    loads = loads.astype(jnp.bfloat16).reshape(N_TILE, N_SUB, N_REP, STEPS, N_TILE, bucket)
    arrived = jnp.transpose(loads, (4, 1, 2, 3, 0, 5))
    area_rows = node_area.reshape(N_TILE, N_SUB, N_REP, 1, N_TILE, bucket)
    weighted = (arrived * area_rows).astype(jnp.bfloat16)
    weighted = jnp.transpose(weighted, (3, 0, 1, 2, 4, 5)).reshape(STEPS, NODES)
    forces = jnp.dot(weighted, mode_shapes, preferred_element_type=jnp.float32)
    modal_accel, modal_state = oscillate(forces, frequency, damping_ratio, modal_start)
    node_accel = jnp.dot(modal_accel.astype(jnp.bfloat16), mode_shapes.T, preferred_element_type=jnp.float32).astype(jnp.bfloat16)
    returned = node_accel.reshape(STEPS, N_TILE, N_SUB, N_REP, N_TILE, bucket)
    returned = jnp.transpose(returned, (4, 2, 3, 0, 1, 5)).reshape(devices, STEPS, SLOTS)
    surface = jnp.einsum("dnt,dst->dns", returned.astype(jnp.float32), routes.astype(jnp.float32))
    surface_accel = surface.astype(jnp.bfloat16).reshape(N_TILE, N_SUB, N_REP, STEPS, SLOTS)
    return grid_now, grid_before, surface_accel, modal_state
```

```python
import functools

import jax
import jax.numpy as jnp
from jax import lax
from jax.experimental import pallas as pl
from jax.experimental.pallas import tpu as pltpu
from jax.sharding import PartitionSpec as P

STEPS = 4
HALO = 4


nonlinear = 0.03
viscous = 0.02


def extended(shard, sides, width):
    for axis, dim in sides:
        count, length = (lax.axis_size(axis), shard.shape[dim])
        up = [(i, (i + 1) % count) for i in range(count - 1)]
        down = [(j, i) for i, j in up]
        last = lax.slice_in_dim(shard, length - width, length, axis=dim)
        first = lax.slice_in_dim(shard, 0, width, axis=dim)
        before = lax.ppermute(last, axis, up)
        after = lax.ppermute(first, axis, down)
        shard = jnp.concatenate([before, shard, after], axis=dim)
    return shard


def laplace(padded):
    middle = padded[1:-1, 1:-1, 1:-1]
    summed = padded[2:, 1:-1, 1:-1] + padded[:-2, 1:-1, 1:-1]
    summed = summed + padded[1:-1, 2:, 1:-1] + padded[1:-1, :-2, 1:-1]
    summed = summed + padded[1:-1, 1:-1, 2:] + padded[1:-1, 1:-1, :-2]
    return summed - 6.0 * middle


def advance(wide_now, wide_before, coefficient):
    current = wide_now[1:-1, 1:-1, 1:-1]
    before = wide_before[1:-1, 1:-1, 1:-1]
    change = current - before
    driving = (
        coefficient * laplace(wide_now)
        + viscous * laplace(wide_now - wide_before)
        + 2.0 * nonlinear * change * change
    )
    return 2.0 * current - before + (1.0 + 2.0 * nonlinear * current) * driving


def routing(owners, live_count, tile_total):
    slot_total = owners.shape[0]
    bucket = slot_total // tile_total
    position = jnp.arange(slot_total, dtype=jnp.int32)
    is_live = position < live_count
    member = (
        (owners[:, None] == jnp.arange(tile_total, dtype=jnp.int32)[None, :]) & is_live[:, None]
    ).astype(jnp.float32)
    earlier = (position[None, :] < position[:, None]).astype(jnp.float32)
    before = jnp.dot(earlier, member, precision=lax.Precision.HIGHEST)
    bucket_rank = jnp.sum(before * member, axis=1).astype(jnp.int32)
    target = owners * bucket + bucket_rank
    return ((target[:, None] == position[None, :]) & is_live[:, None]).astype(jnp.bfloat16)


def oscillate(forces, frequency, damping_ratio, start_state):

    def advance_mode(carried, force_row):
        displace, velocity = carried
        acceleration = (
            force_row
            - 2.0 * damping_ratio * frequency * velocity
            - frequency * frequency * displace
        )
        velocity = velocity + acceleration
        displace = displace + velocity
        return ((displace, velocity), acceleration)

    (displace, velocity), modal_accel = lax.scan(
        advance_mode, (start_state[0], start_state[1]), forces
    )
    return (modal_accel, jnp.stack([displace, velocity]))


def trim_rim(array, depth):
    return array[
        depth : array.shape[0] - depth,
        depth : array.shape[1] - depth,
        depth : array.shape[2] - depth,
    ]


def inside_range(offset, length, axis_devices, margin):
    position = offset * length - margin + jnp.arange(length + 2 * margin, dtype=jnp.int32)
    return ((position >= 0) & (position < axis_devices * length)).astype(jnp.float32)


def body(
    pressure,
    previous_pressure,
    courant_square,
    node_area,
    mode_shapes,
    frequency,
    damping_ratio,
    modal_start,
    slot_cell,
    slot_owner,
    surface_count,
):
    tile_total = lax.axis_size("tile")
    extent_first, extent_second, extent_third = pressure.shape
    slot_total = slot_cell.shape[-1]
    bucket = slot_total // tile_total
    routing_matrix = routing(slot_owner.reshape(slot_total), surface_count.reshape(()), tile_total)
    cell_index = slot_cell.reshape(slot_total)
    fields = jnp.stack([pressure, previous_pressure])
    margin = HALO
    coef_wide = extended(courant_square, (("tile", 0), ("sub", 1), ("rep", 2)), margin)
    inside_first = inside_range(lax.axis_index("tile"), extent_first, lax.axis_size("tile"), margin)
    inside_second = inside_range(lax.axis_index("sub"), extent_second, lax.axis_size("sub"), margin)
    inside_third = inside_range(lax.axis_index("rep"), extent_third, lax.axis_size("rep"), margin)
    inside = (
        inside_first[:, None, None] * inside_second[None, :, None] * inside_third[None, None, :]
    )

    def deep_block(carried, unused):
        padded = extended(carried, (("tile", 1), ("sub", 2), ("rep", 3)), margin)
        recorded = []
        for layer_index in range(margin):
            edge_depth = layer_index + 1
            updated = advance(padded[0], padded[1], trim_rim(coef_wide, edge_depth)) * trim_rim(
                inside, edge_depth
            )
            interior = trim_rim(updated, margin - edge_depth)
            recorded.append(jnp.take(interior.reshape(-1), cell_index).astype(jnp.bfloat16))
            padded = jnp.stack([updated, trim_rim(padded[0], 1)])
        return (padded, jnp.stack(recorded))

    fields, history = lax.scan(deep_block, fields, None, length=STEPS // margin)
    history = history.reshape(STEPS, slot_total)
    final_field = fields[0]
    prior_field = fields[1]
    bucketed = jnp.dot(history, routing_matrix, preferred_element_type=jnp.float32).astype(
        jnp.bfloat16
    )
    bucketed = bucketed.reshape(STEPS, tile_total, bucket)
    arrived = lax.all_to_all(bucketed, "tile", split_axis=1, concat_axis=1, tiled=True)
    arrived_flat = arrived.reshape(arrived.shape[0], slot_total)
    weighted = (arrived_flat * node_area).astype(jnp.bfloat16)
    partial_forces = jnp.dot(weighted, mode_shapes, preferred_element_type=jnp.float32)
    device_total = lax.axis_size("tile") * lax.axis_size("sub") * lax.axis_size("rep")
    mode_count = mode_shapes.shape[1]
    mode_share = mode_count // device_total
    first_mode = lax.axis_index(("tile", "sub", "rep")) * mode_share
    forces = lax.psum_scatter(
        partial_forces, ("tile", "sub", "rep"), scatter_dimension=1, tiled=True
    )
    local_frequency = lax.dynamic_slice_in_dim(frequency, first_mode, mode_share, 0)
    local_damping = lax.dynamic_slice_in_dim(damping_ratio, first_mode, mode_share, 0)
    local_start = lax.dynamic_slice_in_dim(modal_start, first_mode, mode_share, 1)
    modal_accel, modal_state = oscillate(forces, local_frequency, local_damping, local_start)
    modal_rounded = modal_accel.astype(jnp.bfloat16)
    node_accel = lax.dot_general(
        lax.all_gather(modal_rounded, ("tile", "sub", "rep"), axis=1, tiled=True),
        mode_shapes,
        (((1,), (1,)), ((), ())),
        preferred_element_type=jnp.float32,
    )
    outgoing = node_accel.astype(jnp.bfloat16).reshape(STEPS, tile_total, bucket)
    returned = lax.all_to_all(outgoing, "tile", split_axis=1, concat_axis=1, tiled=True)
    surface = lax.dot_general(
        returned.reshape(STEPS, slot_total),
        routing_matrix,
        (((1,), (1,)), ((), ())),
        preferred_element_type=jnp.float32,
    )
    surface_accel = surface.astype(jnp.bfloat16).reshape(1, 1, 1, STEPS, slot_total)
    return (final_field, prior_field, surface_accel, modal_state)

LANES = 128
MESH = pl.DeviceIdType.MESH


def other_devices(tiles, subs, reps):
    return [
        (i, j, k)
        for i in range(tiles)
        for j in range(subs)
        for k in range(reps)
        if (i, j, k) != (0, 0, 0)
    ]


def dot(a, b, contract):
    return lax.dot_general(a, b, ((contract[:1], contract[1:]), ((), ())), preferred_element_type=jnp.float32)


def window_kernel(
    tiles,
    pressure_ref,
    previous_ref,
    courant_ref,
    area_ref,
    modes_hbm,
    frequency_ref,
    damping_ref,
    start_ref,
    cell_ref,
    owner_ref,
    count_ref,
    final_ref,
    prior_ref,
    surface_ref,
    state_ref,
    modes,
    field,
    side_out,
    low,
    high,
    side_in,
    pair_in,
    loads_out,
    loads_in,
    weighted,
    force_out,
    force_in,
    accel_out,
    accel_in,
    back_out,
    back_in,
    modes_sem,
    halo_send,
    halo_recv,
    loads_send,
    loads_recv,
    force_send,
    force_recv,
    accel_send,
    accel_recv,
    back_send,
    back_recv,
):
    t, s, r = lax.axis_index("tile"), lax.axis_index("sub"), lax.axis_index("rep")
    first, second, third = pressure_ref.shape
    slots = cell_ref.shape[1]
    bucket = slots // tiles
    padded_rows = tiles * LANES
    partners = other_devices(tiles, 2, 2)
    share = state_ref.shape[1]
    me = (t * 2 + s) * 2 + r

    def place(offset):
        i, j, k = offset
        return (lax.rem(t + i, tiles), lax.rem(s + j, 2), lax.rem(r + k, 2))

    def ident(where):
        return {"tile": where[0], "sub": where[1], "rep": where[2]}

    def linear(where):
        return (where[0] * 2 + where[1]) * 2 + where[2]

    barrier = pltpu.get_barrier_semaphore()
    for offset in partners:
        pl.semaphore_signal(barrier, inc=1, device_id=ident(place(offset)), device_id_type=MESH)

    mode_copies = [
        pltpu.make_async_copy(
            modes_hbm.at[pl.ds(i * bucket, bucket)],
            modes.at[pl.ds(i * LANES, bucket)],
            modes_sem.at[i],
        )
        for i in range(tiles)
    ]
    for copy in mode_copies:
        copy.start()

    def row(value):
        return jnp.where(s == 0, value[:, second - 1, :], value[:, 0, :])

    p_now, p_before = pressure_ref[...], previous_ref[...]
    side_out[0] = row(p_now)
    side_out[1] = row(p_before)

    def level(k):
        return (pressure_ref, previous_ref)[k] if k < 2 else field.at[k - 2]

    def remote(source, target, sems, index, where):
        return pltpu.make_async_remote_copy(
            src_ref=source,
            dst_ref=target,
            send_sem=sems[0].at[index],
            recv_sem=sems[1].at[index],
            device_id=where,
            device_id_type=MESH,
        )

    halo = (halo_send, halo_recv)

    def up_copy(k):
        return remote(level(k).at[first - 1], low.at[k], halo, (k, 0), {"tile": jnp.minimum(t + 1, tiles - 1)})

    def down_copy(k):
        return remote(level(k).at[0], high.at[k], halo, (k, 1), {"tile": jnp.maximum(t - 1, 0)})

    def side_copy(k):
        return remote(side_out.at[k], side_in.at[k], halo, (k, 2), {"sub": 1 - s})

    def pair_copy(k):
        return remote(level(k), pair_in.at[k], halo, (k, 3), {"rep": 1 - r})

    def send(k):
        @pl.when(t < tiles - 1)
        def _():
            up_copy(k).start()

        @pl.when(t > 0)
        def _():
            down_copy(k).start()

        side_copy(k).start()
        pair_copy(k).start()

    def receive(k):
        @pl.when(t > 0)
        def _():
            up_copy(k).wait_recv()

        @pl.when(t < tiles - 1)
        def _():
            down_copy(k).wait_recv()

        side_copy(k).wait_recv()
        pair_copy(k).wait_recv()

    def sent(k):
        @pl.when(t < tiles - 1)
        def _():
            up_copy(k).wait_send()

        @pl.when(t > 0)
        def _():
            down_copy(k).wait_send()

        side_copy(k).wait_send()
        pair_copy(k).wait_send()

    pl.semaphore_wait(barrier, len(partners))
    send(0)
    send(1)

    for i in range(tiles):
        if bucket < LANES:
            modes[i * LANES + bucket : (i + 1) * LANES, :] = jnp.zeros(
                (LANES - bucket, modes.shape[1]), modes.dtype
            )
    weighted[...] = jnp.zeros_like(weighted)
    owner = owner_ref[...]
    cell = cell_ref[...]
    lane = lax.broadcasted_iota(jnp.int32, (1, slots), 1)
    live = lane < count_ref[...]
    owner_live = jnp.where(live, owner, -1)
    height = -(-tiles // 8) * 8
    member = (
        lax.broadcasted_iota(jnp.int32, (height, slots), 0) == owner_live
    ).astype(jnp.float32)
    earlier = (
        lax.broadcasted_iota(jnp.int32, (slots, slots), 0)
        < lax.broadcasted_iota(jnp.int32, (slots, slots), 1)
    ).astype(jnp.float32).astype(jnp.bfloat16)
    before = dot(member.astype(jnp.bfloat16), earlier, (1, 0))
    rank = jnp.sum(before * member, axis=0, keepdims=True).astype(jnp.int32)
    target = jnp.where(live, owner * LANES + rank, -1)
    route = (
        (lax.broadcasted_iota(jnp.int32, (padded_rows, slots), 0) == target)
        .astype(jnp.float32)
        .astype(jnp.bfloat16)
    )
    row_of = cell // third
    lane_of = cell - row_of * third
    pick_row = (
        (lax.broadcasted_iota(jnp.int32, (first * second, slots), 0) == row_of)
        .astype(jnp.float32)
        .astype(jnp.bfloat16)
    )
    pick_lane = (
        (lax.broadcasted_iota(jnp.int32, (third, slots), 0) == lane_of)
        .astype(jnp.float32)
        .astype(jnp.bfloat16)
    )
    at_row = dot(pick_row, route, (1, 1))
    at_lane = dot(pick_lane, route, (1, 1)).astype(jnp.bfloat16)

    courant = courant_ref[...]
    at_first = lax.broadcasted_iota(jnp.int32, (first, 1, 1), 0)
    at_second = lax.broadcasted_iota(jnp.int32, (1, second, third), 1)
    at_third = lax.broadcasted_iota(jnp.int32, (1, second, third), 2)

    def inner(p):
        total = -6.0 * p
        zero = jnp.zeros((1, second, third), jnp.float32)
        total = total + jnp.concatenate([zero, p[:-1]], axis=0)
        total = total + jnp.concatenate([p[1:], zero], axis=0)
        total = total + jnp.where(at_second == 0, 0.0, pltpu.roll(p, 1, 1))
        total = total + jnp.where(at_second == second - 1, 0.0, pltpu.roll(p, second - 1, 1))
        total = total + jnp.where(at_third == 0, 0.0, pltpu.roll(p, 1, 2))
        total = total + jnp.where(at_third == third - 1, 0.0, pltpu.roll(p, third - 1, 2))
        return total

    def outer(total, k):
        below = jnp.where(t > 0, low[k], 0.0)
        above = jnp.where(t < tiles - 1, high[k], 0.0)
        edge = jnp.where(s == 0, second - 1, 0)
        beside = jnp.where(at_second == edge, side_in[k][:, None, :], 0.0)
        q = pair_in[k]
        lane_edge = jnp.where(r == 0, third - 1, 0)
        shifted = jnp.where(r == 0, pltpu.roll(q, third - 1, 2), pltpu.roll(q, 1, 2))
        across = jnp.where(at_third == lane_edge, shifted, 0.0)
        total = total + beside + across
        return jnp.concatenate(
            [total[:1] + below[None], total[1:-1], total[-1:] + above[None]], axis=0
        )

    lap_part, lap_before_part = inner(p_now), inner(p_before)
    receive(0)
    receive(1)
    lap_before = outer(lap_before_part, 1)
    lap = outer(lap_part, 0)
    steps = STEPS
    for n in range(steps):
        change = p_now - p_before
        driving = (
            courant * lap
            + viscous * (lap - lap_before)
            + 2.0 * nonlinear * change * change
        )
        p_next = 2.0 * p_now - p_before + (1.0 + 2.0 * nonlinear * p_now) * driving
        if n < steps - 1:
            k = n + 2
            field[n] = p_next
            side_out[k] = row(p_next)
            send(k)
        else:
            final_ref[...] = p_next
            prior_ref[...] = p_now
        chosen = dot(
            p_next.reshape(first * second, third).astype(jnp.bfloat16), at_lane, (1, 0)
        )
        picked = jnp.sum(chosen * at_row, axis=0, keepdims=True)
        for i in range(tiles):
            loads_out[i, n : n + 1, :] = picked[:, i * LANES : (i + 1) * LANES]
        if n < steps - 1:
            lap_before = lap
            part = inner(p_next)
            receive(k)
            lap = outer(part, k)
            p_before, p_now = p_now, p_next

    def tile_copy(source, target, sems, i):
        to = lax.rem(t + i, tiles)
        return remote(source.at[to], target.at[t], sems, i, {"tile": to})

    loads_copies = [
        tile_copy(loads_out, loads_in, (loads_send, loads_recv), i) for i in range(1, tiles)
    ]
    for copy in loads_copies[::-1]:
        copy.start()
    loads_in[t] = loads_out[t]
    area = area_ref[...]
    lane_row = lax.broadcasted_iota(jnp.int32, (1, LANES), 1)
    areas = []
    for i in range(tiles):
        moved = pltpu.roll(area, (slots - i * bucket) % slots, 1) if i else area
        areas.append(jnp.where(lane_row < bucket, moved[:, :LANES], 0.0))
    for copy in mode_copies:
        copy.wait()
    for copy in loads_copies:
        copy.wait_recv()
    for i in range(tiles):
        weighted[:steps, i * LANES : (i + 1) * LANES] = loads_in[i] * areas[i]
    forces = dot(weighted[...].astype(jnp.bfloat16), modes[...], (1, 0))
    devices = len(partners) + 1
    for i in range(devices):
        force_out[i] = forces[:steps, i * share : (i + 1) * share]

    force_copies = [
        remote(
            force_out.at[linear(place(offset))],
            force_in.at[i],
            (force_send, force_recv),
            i,
            ident(place(offset)),
        )
        for i, offset in enumerate(partners)
    ]
    for copy in force_copies[::-1]:
        copy.start()
    begin = pl.multiple_of(me * share, LANES)
    frequency = frequency_ref[:, pl.ds(begin, share)]
    damping = damping_ref[:, pl.ds(begin, share)]
    started = start_ref[:, pl.ds(begin, share)]
    displace, velocity = started[0:1], started[1:2]
    total = force_out[me]
    for i, copy in enumerate(force_copies):
        copy.wait_recv()
        total = total + force_in[i]
    for n in range(steps):
        accel = (
            total[n : n + 1]
            - 2.0 * damping * frequency * velocity
            - frequency * frequency * displace
        )
        velocity = velocity + accel
        displace = displace + velocity
        accel_out[n : n + 1, :] = accel.astype(jnp.bfloat16).astype(jnp.float32)
    accel_copies = [
        remote(accel_out, accel_in.at[me], (accel_send, accel_recv), i, ident(place(offset)))
        for i, offset in enumerate(partners)
    ]
    for copy in accel_copies[::-1]:
        copy.start()
    state_ref[0:1, :] = displace
    state_ref[1:2, :] = velocity
    accel_in[me] = accel_out[...]
    for copy in accel_copies:
        copy.wait_recv()
    accels = jnp.concatenate([accel_in[i] for i in range(devices)], axis=1)
    node = dot(accels.astype(jnp.bfloat16), modes[...], (1, 1))
    node = node.astype(jnp.bfloat16).astype(jnp.float32)
    for i in range(tiles):
        back_out[i] = node[:, i * LANES : (i + 1) * LANES]
    back_copies = [
        tile_copy(back_out, back_in, (back_send, back_recv), i) for i in range(1, tiles)
    ]
    for copy in back_copies[::-1]:
        copy.start()
    back_in[t] = back_out[t]
    for k in range(steps + 1):
        sent(k)
    for copy in loads_copies + force_copies + accel_copies:
        copy.wait_send()
    for copy in back_copies:
        copy.wait_recv()
    returned = jnp.concatenate([back_in[i] for i in range(tiles)], axis=1)
    surface = dot(returned.astype(jnp.bfloat16), route, (1, 0))
    surface_ref[...] = surface.astype(jnp.bfloat16)
    for copy in back_copies:
        copy.wait_send()


def fused_body(
    pressure,
    previous_pressure,
    courant_square,
    node_area,
    mode_shapes,
    frequency,
    damping_ratio,
    modal_start,
    slot_cell,
    slot_owner,
    surface_count,
):
    tiles = lax.axis_size("tile")
    devices = tiles * lax.axis_size("sub") * lax.axis_size("rep")
    first, second, third = pressure.shape
    slots = slot_cell.shape[-1]
    modes = mode_shapes.shape[1]
    share = modes // devices
    f32 = jnp.float32
    levels = STEPS + 1
    vmem = pl.BlockSpec(memory_space=pltpu.VMEM)
    dma = pltpu.SemaphoreType.DMA
    outputs = pl.pallas_call(
        functools.partial(window_kernel, tiles),
        out_shape=(
            jax.ShapeDtypeStruct(pressure.shape, f32),
            jax.ShapeDtypeStruct(pressure.shape, f32),
            jax.ShapeDtypeStruct((STEPS, slots), jnp.bfloat16),
            jax.ShapeDtypeStruct((2, share), f32),
        ),
        in_specs=[vmem] * 4 + [pl.BlockSpec(memory_space=pl.ANY)] + [vmem] * 6,
        out_specs=(vmem,) * 4,
        scratch_shapes=[
            pltpu.VMEM((tiles * LANES, modes), mode_shapes.dtype),
            pltpu.VMEM((STEPS - 1, first, second, third), f32),
            pltpu.VMEM((levels, first, third), f32),
            pltpu.VMEM((levels, second, third), f32),
            pltpu.VMEM((levels, second, third), f32),
            pltpu.VMEM((levels, first, third), f32),
            pltpu.VMEM((levels, first, second, third), f32),
            pltpu.VMEM((tiles, STEPS, LANES), f32),
            pltpu.VMEM((tiles, STEPS, LANES), f32),
            pltpu.VMEM((8, tiles * LANES), f32),
            pltpu.VMEM((devices, STEPS, share), f32),
            pltpu.VMEM((devices, STEPS, share), f32),
            pltpu.VMEM((STEPS, share), f32),
            pltpu.VMEM((devices, STEPS, share), f32),
            pltpu.VMEM((tiles, STEPS, LANES), f32),
            pltpu.VMEM((tiles, STEPS, LANES), f32),
            dma((tiles,)),
            dma((levels, 4)),
            dma((levels, 4)),
            dma((tiles,)),
            dma((tiles,)),
            dma((devices,)),
            dma((devices,)),
            dma((devices,)),
            dma((devices,)),
            dma((tiles,)),
            dma((tiles,)),
        ],
        compiler_params=pltpu.CompilerParams(collective_id=0, has_side_effects=True),
        name="window",
    )(
        pressure,
        previous_pressure,
        courant_square,
        node_area.reshape(1, slots),
        mode_shapes,
        frequency.reshape(1, modes),
        damping_ratio.reshape(1, modes),
        modal_start,
        slot_cell.reshape(1, slots),
        slot_owner.reshape(1, slots),
        surface_count.reshape(1, 1),
    )
    final_field, prior_field, surface, state = outputs
    return (final_field, prior_field, surface.reshape(1, 1, 1, STEPS, slots), state)


def pick_body(
    pressure,
    previous_pressure,
    courant_square,
    node_area,
    mode_shapes,
    frequency,
    damping_ratio,
    modal_start,
    slot_cell,
    slot_owner,
    surface_count,
):
    tiles, subs, reps = (lax.axis_size(axis) for axis in ("tile", "sub", "rep"))
    bucket = slot_cell.shape[-1] // tiles
    modes = mode_shapes.shape[1]
    fits = (
        subs == 2
        and reps == 2
        and tiles > 1
        and pressure.shape[2] == LANES
        and pressure.shape[1] % 8 == 0
        and pressure.shape[0] > 1
        and max(pressure.shape[0] * pressure.shape[1], LANES) <= 256
        and bucket <= LANES
        and bucket % 16 == 0
        and slot_cell.shape[-1] % LANES == 0
        and modes % (tiles * subs * reps * LANES) == 0
    )
    return (fused_body if fits else body)(
        pressure,
        previous_pressure,
        courant_square,
        node_area,
        mode_shapes,
        frequency,
        damping_ratio,
        modal_start,
        slot_cell,
        slot_owner,
        surface_count,
    )


def solution(mesh):
    in_specs = (
        P(("groups", "tile"), "sub", "rep"),
        P(("groups", "tile"), "sub", "rep"),
        P(("groups", "tile"), "sub", "rep"),
        P(("groups", "tile", "sub", "rep")),
        P(("groups", "tile", "sub", "rep"), None),
        P("groups"),
        P("groups"),
        P(None, "groups"),
        P(("groups", "tile"), "sub", "rep", None),
        P(("groups", "tile"), "sub", "rep", None, None),
        P(("groups", "sub"), "rep", "tile"),
    )
    out_specs = (
        P(("groups", "tile"), "sub", "rep"),
        P(("groups", "tile"), "sub", "rep"),
        P(("groups", "tile"), "sub", "rep", None, None),
        P(None, ("groups", "tile", "sub", "rep")),
    )
    return jax.shard_map(
        pick_body, mesh=mesh, in_specs=in_specs, out_specs=out_specs, check_vma=False)
```

```python
import functools

import jax
import jax.numpy as jnp
from jax import lax
from jax.experimental import pallas as pl
from jax.experimental.pallas import tpu as pltpu
from jax.sharding import PartitionSpec as P

STEPS = 4
HALO = 4


nonlinear = 0.03
viscous = 0.02


def extended(shard, sides, width):
    for axis, dim in sides:
        count, length = (lax.axis_size(axis), shard.shape[dim])
        up = [(i, (i + 1) % count) for i in range(count - 1)]
        down = [(j, i) for i, j in up]
        last = lax.slice_in_dim(shard, length - width, length, axis=dim)
        first = lax.slice_in_dim(shard, 0, width, axis=dim)
        before = lax.ppermute(last, axis, up)
        after = lax.ppermute(first, axis, down)
        shard = jnp.concatenate([before, shard, after], axis=dim)
    return shard


def laplace(padded):
    middle = padded[1:-1, 1:-1, 1:-1]
    summed = padded[2:, 1:-1, 1:-1] + padded[:-2, 1:-1, 1:-1]
    summed = summed + padded[1:-1, 2:, 1:-1] + padded[1:-1, :-2, 1:-1]
    summed = summed + padded[1:-1, 1:-1, 2:] + padded[1:-1, 1:-1, :-2]
    return summed - 6.0 * middle


def advance(wide_now, wide_before, coefficient):
    current = wide_now[1:-1, 1:-1, 1:-1]
    before = wide_before[1:-1, 1:-1, 1:-1]
    change = current - before
    driving = (
        coefficient * laplace(wide_now)
        + viscous * laplace(wide_now - wide_before)
        + 2.0 * nonlinear * change * change
    )
    return 2.0 * current - before + (1.0 + 2.0 * nonlinear * current) * driving


def routing(owners, live_count, tile_total):
    slot_total = owners.shape[0]
    bucket = slot_total // tile_total
    position = jnp.arange(slot_total, dtype=jnp.int32)
    is_live = position < live_count
    member = (
        (owners[:, None] == jnp.arange(tile_total, dtype=jnp.int32)[None, :]) & is_live[:, None]
    ).astype(jnp.float32)
    earlier = (position[None, :] < position[:, None]).astype(jnp.float32)
    before = jnp.dot(earlier, member, precision=lax.Precision.HIGHEST)
    bucket_rank = jnp.sum(before * member, axis=1).astype(jnp.int32)
    target = owners * bucket + bucket_rank
    return ((target[:, None] == position[None, :]) & is_live[:, None]).astype(jnp.bfloat16)


def oscillate(forces, frequency, damping_ratio, start_state):

    def advance_mode(carried, force_row):
        displace, velocity = carried
        acceleration = (
            force_row
            - 2.0 * damping_ratio * frequency * velocity
            - frequency * frequency * displace
        )
        velocity = velocity + acceleration
        displace = displace + velocity
        return ((displace, velocity), acceleration)

    (displace, velocity), modal_accel = lax.scan(
        advance_mode, (start_state[0], start_state[1]), forces
    )
    return (modal_accel, jnp.stack([displace, velocity]))


def trim_rim(array, depth):
    return array[
        depth : array.shape[0] - depth,
        depth : array.shape[1] - depth,
        depth : array.shape[2] - depth,
    ]


def inside_range(offset, length, axis_devices, margin):
    position = offset * length - margin + jnp.arange(length + 2 * margin, dtype=jnp.int32)
    return ((position >= 0) & (position < axis_devices * length)).astype(jnp.float32)


def body(
    pressure,
    previous_pressure,
    courant_square,
    node_area,
    mode_shapes,
    frequency,
    damping_ratio,
    modal_start,
    slot_cell,
    slot_owner,
    surface_count,
):
    tile_total = lax.axis_size("tile")
    extent_first, extent_second, extent_third = pressure.shape
    slot_total = slot_cell.shape[-1]
    bucket = slot_total // tile_total
    routing_matrix = routing(slot_owner.reshape(slot_total), surface_count.reshape(()), tile_total)
    cell_index = slot_cell.reshape(slot_total)
    fields = jnp.stack([pressure, previous_pressure])
    margin = HALO
    coef_wide = extended(courant_square, (("tile", 0), ("sub", 1), ("rep", 2)), margin)
    inside_first = inside_range(lax.axis_index("tile"), extent_first, lax.axis_size("tile"), margin)
    inside_second = inside_range(lax.axis_index("sub"), extent_second, lax.axis_size("sub"), margin)
    inside_third = inside_range(lax.axis_index("rep"), extent_third, lax.axis_size("rep"), margin)
    inside = (
        inside_first[:, None, None] * inside_second[None, :, None] * inside_third[None, None, :]
    )

    def deep_block(carried, unused):
        padded = extended(carried, (("tile", 1), ("sub", 2), ("rep", 3)), margin)
        recorded = []
        for layer_index in range(margin):
            edge_depth = layer_index + 1
            updated = advance(padded[0], padded[1], trim_rim(coef_wide, edge_depth)) * trim_rim(
                inside, edge_depth
            )
            interior = trim_rim(updated, margin - edge_depth)
            recorded.append(jnp.take(interior.reshape(-1), cell_index).astype(jnp.bfloat16))
            padded = jnp.stack([updated, trim_rim(padded[0], 1)])
        return (padded, jnp.stack(recorded))

    fields, history = lax.scan(deep_block, fields, None, length=STEPS // margin)
    history = history.reshape(STEPS, slot_total)
    final_field = fields[0]
    prior_field = fields[1]
    bucketed = jnp.dot(history, routing_matrix, preferred_element_type=jnp.float32).astype(
        jnp.bfloat16
    )
    bucketed = bucketed.reshape(STEPS, tile_total, bucket)
    arrived = lax.all_to_all(bucketed, "tile", split_axis=1, concat_axis=1, tiled=True)
    arrived_flat = arrived.reshape(arrived.shape[0], slot_total)
    weighted = (arrived_flat * node_area).astype(jnp.bfloat16)
    partial_forces = jnp.dot(weighted, mode_shapes, preferred_element_type=jnp.float32)
    device_total = lax.axis_size("tile") * lax.axis_size("sub") * lax.axis_size("rep")
    mode_count = mode_shapes.shape[1]
    mode_share = mode_count // device_total
    first_mode = lax.axis_index(("tile", "sub", "rep")) * mode_share
    forces = lax.psum_scatter(
        partial_forces, ("tile", "sub", "rep"), scatter_dimension=1, tiled=True
    )
    local_frequency = lax.dynamic_slice_in_dim(frequency, first_mode, mode_share, 0)
    local_damping = lax.dynamic_slice_in_dim(damping_ratio, first_mode, mode_share, 0)
    local_start = lax.dynamic_slice_in_dim(modal_start, first_mode, mode_share, 1)
    modal_accel, modal_state = oscillate(forces, local_frequency, local_damping, local_start)
    modal_rounded = modal_accel.astype(jnp.bfloat16)
    node_accel = lax.dot_general(
        lax.all_gather(modal_rounded, ("tile", "sub", "rep"), axis=1, tiled=True),
        mode_shapes,
        (((1,), (1,)), ((), ())),
        preferred_element_type=jnp.float32,
    )
    outgoing = node_accel.astype(jnp.bfloat16).reshape(STEPS, tile_total, bucket)
    returned = lax.all_to_all(outgoing, "tile", split_axis=1, concat_axis=1, tiled=True)
    surface = lax.dot_general(
        returned.reshape(STEPS, slot_total),
        routing_matrix,
        (((1,), (1,)), ((), ())),
        preferred_element_type=jnp.float32,
    )
    surface_accel = surface.astype(jnp.bfloat16).reshape(1, 1, 1, STEPS, slot_total)
    return (final_field, prior_field, surface_accel, modal_state)

LANES = 128
MESH = pl.DeviceIdType.MESH


def other_devices(tiles, subs, reps):
    return [
        (i, j, k)
        for i in range(tiles)
        for j in range(subs)
        for k in range(reps)
        if (i, j, k) != (0, 0, 0)
    ]


def dot(a, b, contract):
    return lax.dot_general(a, b, ((contract[:1], contract[1:]), ((), ())), preferred_element_type=jnp.float32)


def window_kernel(
    tiles,
    pressure_hbm,
    previous_hbm,
    courant_hbm,
    area_hbm,
    modes_hbm,
    frequency_hbm,
    damping_hbm,
    start_hbm,
    cell_hbm,
    owner_hbm,
    count_hbm,
    final_ref,
    prior_ref,
    surface_ref,
    state_ref,
    pressure_ref,
    previous_ref,
    courant_ref,
    area_ref,
    frequency_ref,
    damping_ref,
    start_ref,
    cell_ref,
    owner_ref,
    count_ref,
    modes,
    field,
    side_out,
    low,
    high,
    side_in,
    pair_in,
    loads_out,
    loads_in,
    weighted,
    force_out,
    force_in,
    accel_out,
    accel_in,
    back_out,
    back_in,
    modes_sem,
    halo_send,
    halo_recv,
    loads_send,
    loads_recv,
    force_send,
    force_recv,
    accel_send,
    accel_recv,
    back_send,
    back_recv,
    input_sem,
):
    t, s, r = lax.axis_index("tile"), lax.axis_index("sub"), lax.axis_index("rep")
    first, second, third = pressure_ref.shape
    slots = cell_ref.shape[1]
    bucket = slots // tiles
    padded_rows = tiles * LANES
    partners = other_devices(tiles, 2, 2)
    share = state_ref.shape[1]
    me = (t * 2 + s) * 2 + r

    def place(offset):
        i, j, k = offset
        return (lax.rem(t + i, tiles), lax.rem(s + j, 2), lax.rem(r + k, 2))

    def ident(where):
        return {"tile": where[0], "sub": where[1], "rep": where[2]}

    def linear(where):
        return (where[0] * 2 + where[1]) * 2 + where[2]

    barrier = pltpu.get_barrier_semaphore()
    for offset in partners:
        pl.semaphore_signal(barrier, inc=1, device_id=ident(place(offset)), device_id_type=MESH)

    mode_copies = [
        pltpu.make_async_copy(
            modes_hbm.at[pl.ds(i * bucket, bucket)],
            modes.at[pl.ds(i * LANES, bucket)],
            modes_sem.at[i],
        )
        for i in range(tiles)
    ]
    inputs = [
        (pressure_hbm, pressure_ref),
        (previous_hbm, previous_ref),
        (courant_hbm, courant_ref),
        (area_hbm, area_ref),
        (frequency_hbm, frequency_ref),
        (damping_hbm, damping_ref),
        (start_hbm, start_ref),
        (cell_hbm, cell_ref),
        (owner_hbm, owner_ref),
        (count_hbm, count_ref),
    ]
    input_copies = [
        pltpu.make_async_copy(source, held, input_sem.at[i])
        for i, (source, held) in enumerate(inputs)
    ]
    for copy in input_copies:
        copy.start()
    for copy in mode_copies:
        copy.start()

    def row(value):
        return jnp.where(s == 0, value[:, second - 1, :], value[:, 0, :])

    for copy in input_copies:
        copy.wait()
    p_now, p_before = pressure_ref[...], previous_ref[...]
    side_out[0] = row(p_now)
    side_out[1] = row(p_before)

    def level(k):
        return (pressure_ref, previous_ref)[k] if k < 2 else field.at[k - 2]

    def remote(source, target, sems, index, where):
        return pltpu.make_async_remote_copy(
            src_ref=source,
            dst_ref=target,
            send_sem=sems[0].at[index],
            recv_sem=sems[1].at[index],
            device_id=where,
            device_id_type=MESH,
        )

    halo = (halo_send, halo_recv)

    def up_copy(k):
        return remote(level(k).at[first - 1], low.at[k], halo, (k, 0), {"tile": jnp.minimum(t + 1, tiles - 1)})

    def down_copy(k):
        return remote(level(k).at[0], high.at[k], halo, (k, 1), {"tile": jnp.maximum(t - 1, 0)})

    def side_copy(k):
        return remote(side_out.at[k], side_in.at[k], halo, (k, 2), {"sub": 1 - s})

    def pair_copy(k):
        return remote(level(k), pair_in.at[k], halo, (k, 3), {"rep": 1 - r})

    def send(k):
        @pl.when(t < tiles - 1)
        def _():
            up_copy(k).start()

        @pl.when(t > 0)
        def _():
            down_copy(k).start()

        side_copy(k).start()
        pair_copy(k).start()

    def receive(k):
        @pl.when(t > 0)
        def _():
            up_copy(k).wait_recv()

        @pl.when(t < tiles - 1)
        def _():
            down_copy(k).wait_recv()

        side_copy(k).wait_recv()
        pair_copy(k).wait_recv()

    def sent(k):
        @pl.when(t < tiles - 1)
        def _():
            up_copy(k).wait_send()

        @pl.when(t > 0)
        def _():
            down_copy(k).wait_send()

        side_copy(k).wait_send()
        pair_copy(k).wait_send()

    pl.semaphore_wait(barrier, len(partners))
    send(0)
    send(1)

    for i in range(tiles):
        if bucket < LANES:
            modes[i * LANES + bucket : (i + 1) * LANES, :] = jnp.zeros(
                (LANES - bucket, modes.shape[1]), modes.dtype
            )
    weighted[...] = jnp.zeros_like(weighted)
    owner = owner_ref[...]
    cell = cell_ref[...]
    lane = lax.broadcasted_iota(jnp.int32, (1, slots), 1)
    live = lane < count_ref[0]
    owner_live = jnp.where(live, owner, -1)
    height = -(-tiles // 8) * 8
    member = (
        lax.broadcasted_iota(jnp.int32, (height, slots), 0) == owner_live
    ).astype(jnp.float32)
    earlier = (
        lax.broadcasted_iota(jnp.int32, (slots, slots), 0)
        < lax.broadcasted_iota(jnp.int32, (slots, slots), 1)
    ).astype(jnp.float32).astype(jnp.bfloat16)
    before = dot(member.astype(jnp.bfloat16), earlier, (1, 0))
    rank = jnp.sum(before * member, axis=0, keepdims=True).astype(jnp.int32)
    target = jnp.where(live, owner * LANES + rank, -1)
    route = (
        (lax.broadcasted_iota(jnp.int32, (padded_rows, slots), 0) == target)
        .astype(jnp.float32)
        .astype(jnp.bfloat16)
    )
    row_of = cell // third
    lane_of = cell - row_of * third
    pick_row = (
        (lax.broadcasted_iota(jnp.int32, (first * second, slots), 0) == row_of)
        .astype(jnp.float32)
        .astype(jnp.bfloat16)
    )
    pick_lane = (
        (lax.broadcasted_iota(jnp.int32, (third, slots), 0) == lane_of)
        .astype(jnp.float32)
        .astype(jnp.bfloat16)
    )
    at_row = dot(pick_row, route, (1, 1))
    at_lane = dot(pick_lane, route, (1, 1)).astype(jnp.bfloat16)

    courant = courant_ref[...]
    at_first = lax.broadcasted_iota(jnp.int32, (first, 1, 1), 0)
    at_second = lax.broadcasted_iota(jnp.int32, (1, second, third), 1)
    at_third = lax.broadcasted_iota(jnp.int32, (1, second, third), 2)

    def inner(p):
        total = -6.0 * p
        zero = jnp.zeros((1, second, third), jnp.float32)
        total = total + jnp.concatenate([zero, p[:-1]], axis=0)
        total = total + jnp.concatenate([p[1:], zero], axis=0)
        total = total + jnp.where(at_second == 0, 0.0, pltpu.roll(p, 1, 1))
        total = total + jnp.where(at_second == second - 1, 0.0, pltpu.roll(p, second - 1, 1))
        total = total + jnp.where(at_third == 0, 0.0, pltpu.roll(p, 1, 2))
        total = total + jnp.where(at_third == third - 1, 0.0, pltpu.roll(p, third - 1, 2))
        return total

    def outer(total, k):
        below = jnp.where(t > 0, low[k], 0.0)
        above = jnp.where(t < tiles - 1, high[k], 0.0)
        edge = jnp.where(s == 0, second - 1, 0)
        beside = jnp.where(at_second == edge, side_in[k][:, None, :], 0.0)
        q = pair_in[k]
        lane_edge = jnp.where(r == 0, third - 1, 0)
        shifted = jnp.where(r == 0, pltpu.roll(q, third - 1, 2), pltpu.roll(q, 1, 2))
        across = jnp.where(at_third == lane_edge, shifted, 0.0)
        total = total + beside + across
        return jnp.concatenate(
            [total[:1] + below[None], total[1:-1], total[-1:] + above[None]], axis=0
        )

    lap_part, lap_before_part = inner(p_now), inner(p_before)
    receive(0)
    receive(1)
    lap_before = outer(lap_before_part, 1)
    lap = outer(lap_part, 0)
    steps = STEPS
    for n in range(steps):
        change = p_now - p_before
        driving = (
            courant * lap
            + viscous * (lap - lap_before)
            + 2.0 * nonlinear * change * change
        )
        p_next = 2.0 * p_now - p_before + (1.0 + 2.0 * nonlinear * p_now) * driving
        if n < steps - 1:
            k = n + 2
            field[n] = p_next
            side_out[k] = row(p_next)
            send(k)
        else:
            final_ref[...] = p_next
            prior_ref[...] = p_now
        chosen = dot(
            p_next.reshape(first * second, third).astype(jnp.bfloat16), at_lane, (1, 0)
        )
        picked = jnp.sum(chosen * at_row, axis=0, keepdims=True)
        for i in range(tiles):
            loads_out[i, n : n + 1, :] = picked[:, i * LANES : (i + 1) * LANES]
        if n < steps - 1:
            lap_before = lap
            part = inner(p_next)
            receive(k)
            lap = outer(part, k)
            p_before, p_now = p_now, p_next

    def tile_copy(source, target, sems, i):
        to = lax.rem(t + i, tiles)
        return remote(source.at[to], target.at[t], sems, i, {"tile": to})

    loads_copies = [
        tile_copy(loads_out, loads_in, (loads_send, loads_recv), i) for i in range(1, tiles)
    ]
    for copy in loads_copies[::-1]:
        copy.start()
    loads_in[t] = loads_out[t]
    area = area_ref[...].reshape(1, slots)
    lane_row = lax.broadcasted_iota(jnp.int32, (1, LANES), 1)
    areas = []
    for i in range(tiles):
        moved = pltpu.roll(area, (slots - i * bucket) % slots, 1) if i else area
        areas.append(jnp.where(lane_row < bucket, moved[:, :LANES], 0.0))
    for copy in mode_copies:
        copy.wait()
    for copy in loads_copies:
        copy.wait_recv()
    for i in range(tiles):
        weighted[:steps, i * LANES : (i + 1) * LANES] = loads_in[i] * areas[i]
    forces = dot(weighted[...].astype(jnp.bfloat16), modes[...], (1, 0))
    devices = len(partners) + 1
    for i in range(devices):
        force_out[i] = forces[:steps, i * share : (i + 1) * share]

    force_copies = [
        remote(
            force_out.at[linear(place(offset))],
            force_in.at[i],
            (force_send, force_recv),
            i,
            ident(place(offset)),
        )
        for i, offset in enumerate(partners)
    ]
    for copy in force_copies[::-1]:
        copy.start()
    begin = pl.multiple_of(me * share, LANES)
    frequency = frequency_ref[:, pl.ds(begin, share)]
    damping = damping_ref[:, pl.ds(begin, share)]
    started = start_ref[:, pl.ds(begin, share)]
    displace, velocity = started[0:1], started[1:2]
    total = force_out[me]
    for i, copy in enumerate(force_copies):
        copy.wait_recv()
        total = total + force_in[i]
    for n in range(steps):
        accel = (
            total[n : n + 1]
            - 2.0 * damping * frequency * velocity
            - frequency * frequency * displace
        )
        velocity = velocity + accel
        displace = displace + velocity
        accel_out[n : n + 1, :] = accel.astype(jnp.bfloat16).astype(jnp.float32)
    accel_copies = [
        remote(accel_out, accel_in.at[me], (accel_send, accel_recv), i, ident(place(offset)))
        for i, offset in enumerate(partners)
    ]
    for copy in accel_copies[::-1]:
        copy.start()
    state_ref[0:1, :] = displace
    state_ref[1:2, :] = velocity
    accel_in[me] = accel_out[...]
    for copy in accel_copies:
        copy.wait_recv()
    accels = jnp.concatenate([accel_in[i] for i in range(devices)], axis=1)
    node = dot(accels.astype(jnp.bfloat16), modes[...], (1, 1))
    node = node.astype(jnp.bfloat16).astype(jnp.float32)
    for i in range(tiles):
        back_out[i] = node[:, i * LANES : (i + 1) * LANES]
    back_copies = [
        tile_copy(back_out, back_in, (back_send, back_recv), i) for i in range(1, tiles)
    ]
    for copy in back_copies[::-1]:
        copy.start()
    back_in[t] = back_out[t]
    for k in range(steps + 1):
        sent(k)
    for copy in loads_copies + force_copies + accel_copies:
        copy.wait_send()
    for copy in back_copies:
        copy.wait_recv()
    returned = jnp.concatenate([back_in[i] for i in range(tiles)], axis=1)
    surface = dot(returned.astype(jnp.bfloat16), route, (1, 0))
    surface_ref[...] = surface.astype(jnp.bfloat16)
    for copy in back_copies:
        copy.wait_send()


def place_kernel(*refs):
    sources, targets, sems = refs[:4], refs[4:8], refs[8]
    copies = [
        pltpu.make_async_copy(source, target, sems.at[i])
        for i, (source, target) in enumerate(zip(sources, targets))
    ]
    for copy in copies:
        copy.start()
    for copy in copies:
        copy.wait()


def fused_body(
    pressure,
    previous_pressure,
    courant_square,
    node_area,
    mode_shapes,
    frequency,
    damping_ratio,
    modal_start,
    slot_cell,
    slot_owner,
    surface_count,
):
    tiles = lax.axis_size("tile")
    devices = tiles * lax.axis_size("sub") * lax.axis_size("rep")
    first, second, third = pressure.shape
    slots = slot_cell.shape[-1]
    modes = mode_shapes.shape[1]
    share = modes // devices
    f32 = jnp.float32
    levels = STEPS + 1
    vmem = pl.BlockSpec(memory_space=pltpu.VMEM)
    dma = pltpu.SemaphoreType.DMA
    shapes = (
        jax.ShapeDtypeStruct(pressure.shape, f32),
        jax.ShapeDtypeStruct(pressure.shape, f32),
        jax.ShapeDtypeStruct((STEPS, slots), jnp.bfloat16),
        jax.ShapeDtypeStruct((2, share), f32),
    )
    outputs = pl.pallas_call(
        functools.partial(window_kernel, tiles),
        out_shape=tuple(pltpu.VMEM(shape.shape, shape.dtype) for shape in shapes),
        in_specs=[pl.BlockSpec(memory_space=pl.ANY)] * 11,
        out_specs=(vmem,) * 4,
        scratch_shapes=[
            pltpu.VMEM(pressure.shape, f32),
            pltpu.VMEM(pressure.shape, f32),
            pltpu.VMEM(pressure.shape, f32),
            pltpu.VMEM(node_area.shape, f32),
            pltpu.VMEM((1, modes), f32),
            pltpu.VMEM((1, modes), f32),
            pltpu.VMEM((2, modes), f32),
            pltpu.VMEM((1, slots), jnp.int32),
            pltpu.VMEM((1, slots), jnp.int32),
            pltpu.VMEM((1, 1, 1), jnp.int32),
            pltpu.VMEM((tiles * LANES, modes), mode_shapes.dtype),
            pltpu.VMEM((STEPS - 1, first, second, third), f32),
            pltpu.VMEM((levels, first, third), f32),
            pltpu.VMEM((levels, second, third), f32),
            pltpu.VMEM((levels, second, third), f32),
            pltpu.VMEM((levels, first, third), f32),
            pltpu.VMEM((levels, first, second, third), f32),
            pltpu.VMEM((tiles, STEPS, LANES), f32),
            pltpu.VMEM((tiles, STEPS, LANES), f32),
            pltpu.VMEM((8, tiles * LANES), f32),
            pltpu.VMEM((devices, STEPS, share), f32),
            pltpu.VMEM((devices, STEPS, share), f32),
            pltpu.VMEM((STEPS, share), f32),
            pltpu.VMEM((devices, STEPS, share), f32),
            pltpu.VMEM((tiles, STEPS, LANES), f32),
            pltpu.VMEM((tiles, STEPS, LANES), f32),
            dma((tiles,)),
            dma((levels, 4)),
            dma((levels, 4)),
            dma((tiles,)),
            dma((tiles,)),
            dma((devices,)),
            dma((devices,)),
            dma((devices,)),
            dma((devices,)),
            dma((tiles,)),
            dma((tiles,)),
            dma((10,)),
        ],
        compiler_params=pltpu.CompilerParams(collective_id=0, has_side_effects=True),
        name="window",
    )(
        pressure,
        previous_pressure,
        courant_square,
        node_area,
        mode_shapes,
        frequency.reshape(1, modes),
        damping_ratio.reshape(1, modes),
        modal_start,
        slot_cell.reshape(1, slots),
        slot_owner.reshape(1, slots),
        surface_count,
    )
    final_field, prior_field, surface, state = pl.pallas_call(
        place_kernel,
        out_shape=shapes,
        in_specs=[vmem] * 4,
        out_specs=(pl.BlockSpec(memory_space=pl.ANY),) * 4,
        scratch_shapes=[dma((4,))],
        name="placed",
    )(*(pltpu.with_memory_space_constraint(x, pltpu.VMEM) for x in outputs))
    return (final_field, prior_field, surface.reshape(1, 1, 1, STEPS, slots), state)


def pick_body(
    pressure,
    previous_pressure,
    courant_square,
    node_area,
    mode_shapes,
    frequency,
    damping_ratio,
    modal_start,
    slot_cell,
    slot_owner,
    surface_count,
):
    tiles, subs, reps = (lax.axis_size(axis) for axis in ("tile", "sub", "rep"))
    bucket = slot_cell.shape[-1] // tiles
    modes = mode_shapes.shape[1]
    fits = (
        subs == 2
        and reps == 2
        and tiles > 1
        and pressure.shape[2] == LANES
        and pressure.shape[1] % 8 == 0
        and pressure.shape[0] > 1
        and max(pressure.shape[0] * pressure.shape[1], LANES) <= 256
        and bucket <= LANES
        and bucket % 16 == 0
        and slot_cell.shape[-1] % LANES == 0
        and modes % (tiles * subs * reps * LANES) == 0
    )
    return (fused_body if fits else body)(
        pressure,
        previous_pressure,
        courant_square,
        node_area,
        mode_shapes,
        frequency,
        damping_ratio,
        modal_start,
        slot_cell,
        slot_owner,
        surface_count,
    )


def solution(mesh):
    in_specs = (
        P(("groups", "tile"), "sub", "rep"),
        P(("groups", "tile"), "sub", "rep"),
        P(("groups", "tile"), "sub", "rep"),
        P(("groups", "tile", "sub", "rep")),
        P(("groups", "tile", "sub", "rep"), None),
        P("groups"),
        P("groups"),
        P(None, "groups"),
        P(("groups", "tile"), "sub", "rep", None),
        P(("groups", "tile"), "sub", "rep", None, None),
        P(("groups", "sub"), "rep", "tile"),
    )
    out_specs = (
        P(("groups", "tile"), "sub", "rep"),
        P(("groups", "tile"), "sub", "rep"),
        P(("groups", "tile"), "sub", "rep", None, None),
        P(None, ("groups", "tile", "sub", "rep")),
    )
    return jax.shard_map(
        pick_body, mesh=mesh, in_specs=in_specs, out_specs=out_specs, check_vma=False)
```

```python
import functools

import jax
import jax.numpy as jnp
from jax import lax
from jax.experimental import pallas as pl
from jax.experimental.pallas import tpu as pltpu
from jax.sharding import PartitionSpec as P

STEPS = 4
HALO = 4


nonlinear = 0.03
viscous = 0.02


def extended(shard, sides, width):
    for axis, dim in sides:
        count, length = (lax.axis_size(axis), shard.shape[dim])
        up = [(i, (i + 1) % count) for i in range(count - 1)]
        down = [(j, i) for i, j in up]
        last = lax.slice_in_dim(shard, length - width, length, axis=dim)
        first = lax.slice_in_dim(shard, 0, width, axis=dim)
        before = lax.ppermute(last, axis, up)
        after = lax.ppermute(first, axis, down)
        shard = jnp.concatenate([before, shard, after], axis=dim)
    return shard


def laplace(padded):
    middle = padded[1:-1, 1:-1, 1:-1]
    summed = padded[2:, 1:-1, 1:-1] + padded[:-2, 1:-1, 1:-1]
    summed = summed + padded[1:-1, 2:, 1:-1] + padded[1:-1, :-2, 1:-1]
    summed = summed + padded[1:-1, 1:-1, 2:] + padded[1:-1, 1:-1, :-2]
    return summed - 6.0 * middle


def advance(wide_now, wide_before, coefficient):
    current = wide_now[1:-1, 1:-1, 1:-1]
    before = wide_before[1:-1, 1:-1, 1:-1]
    change = current - before
    driving = (
        coefficient * laplace(wide_now)
        + viscous * laplace(wide_now - wide_before)
        + 2.0 * nonlinear * change * change
    )
    return 2.0 * current - before + (1.0 + 2.0 * nonlinear * current) * driving


def routing(owners, live_count, tile_total):
    slot_total = owners.shape[0]
    bucket = slot_total // tile_total
    position = jnp.arange(slot_total, dtype=jnp.int32)
    is_live = position < live_count
    member = (
        (owners[:, None] == jnp.arange(tile_total, dtype=jnp.int32)[None, :]) & is_live[:, None]
    ).astype(jnp.float32)
    earlier = (position[None, :] < position[:, None]).astype(jnp.float32)
    before = jnp.dot(earlier, member, precision=lax.Precision.HIGHEST)
    bucket_rank = jnp.sum(before * member, axis=1).astype(jnp.int32)
    target = owners * bucket + bucket_rank
    return ((target[:, None] == position[None, :]) & is_live[:, None]).astype(jnp.bfloat16)


def oscillate(forces, frequency, damping_ratio, start_state):

    def advance_mode(carried, force_row):
        displace, velocity = carried
        acceleration = (
            force_row
            - 2.0 * damping_ratio * frequency * velocity
            - frequency * frequency * displace
        )
        velocity = velocity + acceleration
        displace = displace + velocity
        return ((displace, velocity), acceleration)

    (displace, velocity), modal_accel = lax.scan(
        advance_mode, (start_state[0], start_state[1]), forces
    )
    return (modal_accel, jnp.stack([displace, velocity]))


def trim_rim(array, depth):
    return array[
        depth : array.shape[0] - depth,
        depth : array.shape[1] - depth,
        depth : array.shape[2] - depth,
    ]


def inside_range(offset, length, axis_devices, margin):
    position = offset * length - margin + jnp.arange(length + 2 * margin, dtype=jnp.int32)
    return ((position >= 0) & (position < axis_devices * length)).astype(jnp.float32)


def body(
    pressure,
    previous_pressure,
    courant_square,
    node_area,
    mode_shapes,
    frequency,
    damping_ratio,
    modal_start,
    slot_cell,
    slot_owner,
    surface_count,
):
    tile_total = lax.axis_size("tile")
    extent_first, extent_second, extent_third = pressure.shape
    slot_total = slot_cell.shape[-1]
    bucket = slot_total // tile_total
    routing_matrix = routing(slot_owner.reshape(slot_total), surface_count.reshape(()), tile_total)
    cell_index = slot_cell.reshape(slot_total)
    fields = jnp.stack([pressure, previous_pressure])
    margin = HALO
    coef_wide = extended(courant_square, (("tile", 0), ("sub", 1), ("rep", 2)), margin)
    inside_first = inside_range(lax.axis_index("tile"), extent_first, lax.axis_size("tile"), margin)
    inside_second = inside_range(lax.axis_index("sub"), extent_second, lax.axis_size("sub"), margin)
    inside_third = inside_range(lax.axis_index("rep"), extent_third, lax.axis_size("rep"), margin)
    inside = (
        inside_first[:, None, None] * inside_second[None, :, None] * inside_third[None, None, :]
    )

    def deep_block(carried, unused):
        padded = extended(carried, (("tile", 1), ("sub", 2), ("rep", 3)), margin)
        recorded = []
        for layer_index in range(margin):
            edge_depth = layer_index + 1
            updated = advance(padded[0], padded[1], trim_rim(coef_wide, edge_depth)) * trim_rim(
                inside, edge_depth
            )
            interior = trim_rim(updated, margin - edge_depth)
            recorded.append(jnp.take(interior.reshape(-1), cell_index).astype(jnp.bfloat16))
            padded = jnp.stack([updated, trim_rim(padded[0], 1)])
        return (padded, jnp.stack(recorded))

    fields, history = lax.scan(deep_block, fields, None, length=STEPS // margin)
    history = history.reshape(STEPS, slot_total)
    final_field = fields[0]
    prior_field = fields[1]
    bucketed = jnp.dot(history, routing_matrix, preferred_element_type=jnp.float32).astype(
        jnp.bfloat16
    )
    bucketed = bucketed.reshape(STEPS, tile_total, bucket)
    arrived = lax.all_to_all(bucketed, "tile", split_axis=1, concat_axis=1, tiled=True)
    arrived_flat = arrived.reshape(arrived.shape[0], slot_total)
    weighted = (arrived_flat * node_area).astype(jnp.bfloat16)
    partial_forces = jnp.dot(weighted, mode_shapes, preferred_element_type=jnp.float32)
    device_total = lax.axis_size("tile") * lax.axis_size("sub") * lax.axis_size("rep")
    mode_count = mode_shapes.shape[1]
    mode_share = mode_count // device_total
    first_mode = lax.axis_index(("tile", "sub", "rep")) * mode_share
    forces = lax.psum_scatter(
        partial_forces, ("tile", "sub", "rep"), scatter_dimension=1, tiled=True
    )
    local_frequency = lax.dynamic_slice_in_dim(frequency, first_mode, mode_share, 0)
    local_damping = lax.dynamic_slice_in_dim(damping_ratio, first_mode, mode_share, 0)
    local_start = lax.dynamic_slice_in_dim(modal_start, first_mode, mode_share, 1)
    modal_accel, modal_state = oscillate(forces, local_frequency, local_damping, local_start)
    modal_rounded = modal_accel.astype(jnp.bfloat16)
    node_accel = lax.dot_general(
        lax.all_gather(modal_rounded, ("tile", "sub", "rep"), axis=1, tiled=True),
        mode_shapes,
        (((1,), (1,)), ((), ())),
        preferred_element_type=jnp.float32,
    )
    outgoing = node_accel.astype(jnp.bfloat16).reshape(STEPS, tile_total, bucket)
    returned = lax.all_to_all(outgoing, "tile", split_axis=1, concat_axis=1, tiled=True)
    surface = lax.dot_general(
        returned.reshape(STEPS, slot_total),
        routing_matrix,
        (((1,), (1,)), ((), ())),
        preferred_element_type=jnp.float32,
    )
    surface_accel = surface.astype(jnp.bfloat16).reshape(1, 1, 1, STEPS, slot_total)
    return (final_field, prior_field, surface_accel, modal_state)

LANES = 128
MESH = pl.DeviceIdType.MESH


def other_devices(tiles, subs, reps):
    return [
        (i, j, k)
        for i in range(tiles)
        for j in range(subs)
        for k in range(reps)
        if (i, j, k) != (0, 0, 0)
    ]


def dot(a, b, contract):
    return lax.dot_general(a, b, ((contract[:1], contract[1:]), ((), ())), preferred_element_type=jnp.float32)


def window_kernel(
    tiles,
    pressure_hbm,
    previous_hbm,
    courant_hbm,
    area_hbm,
    modes_hbm,
    frequency_hbm,
    damping_hbm,
    start_hbm,
    cell_hbm,
    owner_hbm,
    count_hbm,
    final_ref,
    prior_ref,
    surface_ref,
    state_ref,
    pressure_ref,
    previous_ref,
    courant_ref,
    area_ref,
    frequency_ref,
    damping_ref,
    start_ref,
    cell_ref,
    owner_ref,
    count_ref,
    modes,
    field,
    side_out,
    corner_out,
    low,
    high,
    side_in,
    pair_in,
    corner_in,
    layer_in,
    across_in,
    loads_out,
    loads_in,
    weighted,
    force_out,
    force_in,
    accel_out,
    accel_in,
    back_out,
    back_in,
    modes_sem,
    halo_send,
    halo_recv,
    loads_send,
    loads_recv,
    force_send,
    force_recv,
    accel_send,
    accel_recv,
    back_send,
    back_recv,
    input_sem,
):
    t, s, r = lax.axis_index("tile"), lax.axis_index("sub"), lax.axis_index("rep")
    first, second, third = pressure_ref.shape
    slots = cell_ref.shape[1]
    bucket = slots // tiles
    padded_rows = tiles * LANES
    partners = other_devices(tiles, 2, 2)
    share = state_ref.shape[1]
    me = (t * 2 + s) * 2 + r

    def place(offset):
        i, j, k = offset
        return (lax.rem(t + i, tiles), lax.rem(s + j, 2), lax.rem(r + k, 2))

    def ident(where):
        return {"tile": where[0], "sub": where[1], "rep": where[2]}

    def linear(where):
        return (where[0] * 2 + where[1]) * 2 + where[2]

    barrier = pltpu.get_barrier_semaphore()
    for offset in partners:
        pl.semaphore_signal(barrier, inc=1, device_id=ident(place(offset)), device_id_type=MESH)

    mode_copies = [
        pltpu.make_async_copy(
            modes_hbm.at[pl.ds(i * bucket, bucket)],
            modes.at[pl.ds(i * LANES, bucket)],
            modes_sem.at[i],
        )
        for i in range(tiles)
    ]
    inputs = [
        (pressure_hbm, pressure_ref),
        (previous_hbm, previous_ref),
        (courant_hbm, courant_ref),
        (area_hbm, area_ref),
        (frequency_hbm, frequency_ref),
        (damping_hbm, damping_ref),
        (start_hbm, start_ref),
        (cell_hbm, cell_ref),
        (owner_hbm, owner_ref),
        (count_hbm, count_ref),
    ]
    input_copies = [
        pltpu.make_async_copy(source, held, input_sem.at[i])
        for i, (source, held) in enumerate(inputs)
    ]
    for copy in input_copies:
        copy.start()
    for copy in mode_copies:
        copy.start()

    def near(value):
        return jnp.where(s == 0, value[:, second - 1, :], value[:, 0, :])

    def next_near(value):
        return jnp.where(s == 0, value[:, second - 2, :], value[:, 1, :])

    def stage(k, value):
        rows = near(value)
        side_out[k, 0] = rows
        side_out[k, 1] = next_near(value)
        corner_out[k, 0] = rows[:1]
        corner_out[k, 1] = rows[first - 1 :]

    for copy in input_copies:
        copy.wait()
    p_now, p_before = pressure_ref[...], previous_ref[...]
    courant = courant_ref[...]
    stage(0, p_now)
    stage(1, p_before)
    stage(4, courant)

    def level(k):
        return (pressure_ref, previous_ref, field.at[0], field.at[1], courant_ref)[k]

    def remote(source, target, sems, index, where):
        return pltpu.make_async_remote_copy(
            src_ref=source,
            dst_ref=target,
            send_sem=sems[0].at[index],
            recv_sem=sems[1].at[index],
            device_id=where,
            device_id_type=MESH,
        )

    up = {"tile": jnp.minimum(t + 1, tiles - 1)}
    down = {"tile": jnp.maximum(t - 1, 0)}
    beside_me, pair = {"sub": 1 - s}, {"rep": 1 - r}

    def piece(k, m):
        source, target, where = (
            (level(k).at[pl.ds(first - 2, 2)], low.at[k], up),
            (level(k).at[pl.ds(0, 2)], high.at[k], down),
            (side_out.at[k], side_in.at[k], beside_me),
            (level(k), pair_in.at[k], pair),
            (corner_out.at[k, 1], corner_in.at[k, 0], up | beside_me),
            (corner_out.at[k, 0], corner_in.at[k, 1], down | beside_me),
            (level(k).at[first - 1], layer_in.at[k, 0], up | pair),
            (level(k).at[0], layer_in.at[k, 1], down | pair),
            (side_out.at[k, 0], across_in.at[k], beside_me | pair),
        )[m]
        return remote(source, target, (halo_send, halo_recv), (k, m), where)

    def pieces(k):
        return (0, 1, 2, 3) if k == 4 else (0, 1, 6, 7, 4, 5, 8, 2, 3)

    def each(ks, upward, act):
        todo = [(k, m) for k in ks for m in pieces(k)]

        def run(chosen):
            for k, m in todo:
                if m in chosen:
                    act(piece(k, m))

        @pl.when(t < tiles - 1)
        def _():
            run((0, 4, 6) if upward else (1, 5, 7))

        @pl.when(t > 0)
        def _():
            run((1, 5, 7) if upward else (0, 4, 6))

        run((2, 3, 8))

    def send(ks):
        each(ks, True, lambda copy: copy.start())

    def receive(ks):
        each(ks, False, lambda copy: copy.wait_recv())

    def sent(ks):
        each(ks, True, lambda copy: copy.wait_send())

    pl.semaphore_wait(barrier, len(partners))
    send((0, 1, 4))

    for i in range(tiles):
        if bucket < LANES:
            modes[i * LANES + bucket : (i + 1) * LANES, :] = jnp.zeros(
                (LANES - bucket, modes.shape[1]), modes.dtype
            )
    weighted[...] = jnp.zeros_like(weighted)
    owner = owner_ref[...]
    cell = cell_ref[...]
    lane = lax.broadcasted_iota(jnp.int32, (1, slots), 1)
    live = lane < count_ref[0]
    owner_live = jnp.where(live, owner, -1)
    height = -(-tiles // 8) * 8
    member = (
        lax.broadcasted_iota(jnp.int32, (height, slots), 0) == owner_live
    ).astype(jnp.float32)
    earlier = (
        lax.broadcasted_iota(jnp.int32, (slots, slots), 0)
        < lax.broadcasted_iota(jnp.int32, (slots, slots), 1)
    ).astype(jnp.float32).astype(jnp.bfloat16)
    before = dot(member.astype(jnp.bfloat16), earlier, (1, 0))
    rank = jnp.sum(before * member, axis=0, keepdims=True).astype(jnp.int32)
    target = jnp.where(live, owner * LANES + rank, -1)
    route = (
        (lax.broadcasted_iota(jnp.int32, (padded_rows, slots), 0) == target)
        .astype(jnp.float32)
        .astype(jnp.bfloat16)
    )
    row_of = cell // third
    lane_of = cell - row_of * third
    pick_row = (
        (lax.broadcasted_iota(jnp.int32, (first * second, slots), 0) == row_of)
        .astype(jnp.float32)
        .astype(jnp.bfloat16)
    )
    pick_lane = (
        (lax.broadcasted_iota(jnp.int32, (third, slots), 0) == lane_of)
        .astype(jnp.float32)
        .astype(jnp.bfloat16)
    )
    at_row = dot(pick_row, route, (1, 1))
    at_lane = dot(pick_lane, route, (1, 1)).astype(jnp.bfloat16)

    at_second = lax.broadcasted_iota(jnp.int32, (1, second, third), 1)
    at_third = lax.broadcasted_iota(jnp.int32, (1, 1, third), 2)
    edge_row = jnp.where(s == 0, second - 1, 0)

    def along_lanes(p, q, half, lanes):
        axis = p.ndim - 1
        total = jnp.where(lanes == 0, 0.0, pltpu.roll(p, 1, axis))
        total = total + jnp.where(lanes == third - 1, 0.0, pltpu.roll(p, third - 1, axis))
        edge = jnp.where(half == 0, third - 1, 0)
        shifted = jnp.where(half == 0, pltpu.roll(q, third - 1, axis), pltpu.roll(q, 1, axis))
        return total + jnp.where(lanes == edge, shifted, 0.0)

    def lap_block(p, below, above, beside, q, half):
        total = along_lanes(p, q, half, at_third) - 6.0 * p
        if p.shape[0] > 1:
            below = jnp.concatenate([below, p[:-1]], axis=0)
            above = jnp.concatenate([p[1:], above], axis=0)
        total = total + below + above
        total = total + jnp.where(at_second == 0, 0.0, pltpu.roll(p, 1, 1))
        total = total + jnp.where(at_second == second - 1, 0.0, pltpu.roll(p, second - 1, 1))
        return total + jnp.where(at_second == edge_row, beside[:, None, :], 0.0)

    at_layer = lax.broadcasted_iota(jnp.int32, (first, third), 0)
    at_lane_side = lax.broadcasted_iota(jnp.int32, (1, third), 1)

    def lap_side(g, inward, outward, below, above, q):
        total = along_lanes(g, q, r, at_lane_side) - 6.0 * g
        total = total + inward + outward
        total = total + jnp.where(at_layer == 0, below, pltpu.roll(g, 1, 0))
        return total + jnp.where(at_layer == first - 1, above, pltpu.roll(g, first - 1, 0))

    has_below, has_above = t > 0, t < tiles - 1

    def arrived(k):
        return dict(
            low=jnp.where(has_below, low[k], 0.0),
            high=jnp.where(has_above, high[k], 0.0),
            side=side_in[k],
            pair=pair_in[k],
            corner_low=jnp.where(has_below, corner_in[k, 0], 0.0),
            corner_high=jnp.where(has_above, corner_in[k, 1], 0.0),
            layer_low=jnp.where(has_below, layer_in[k, 0], 0.0)[None],
            layer_high=jnp.where(has_above, layer_in[k, 1], 0.0)[None],
            across=across_in[k],
        )

    def lap_own(p, h):
        return lap_block(p, h["low"][1:], h["high"][:1], h["side"][0], h["pair"], r)

    def lap_rim(p, h):
        low_rim = lap_block(
            h["low"][1:], h["low"][:1], p[:1], h["corner_low"], h["layer_low"], r
        )
        high_rim = lap_block(
            h["high"][:1], p[first - 1 :], h["high"][1:], h["corner_high"], h["layer_high"], r
        )
        side_rim = lap_side(
            h["side"][0], near(p), h["side"][1], h["corner_low"], h["corner_high"], h["across"]
        )
        pair_rim = lap_block(h["pair"], h["layer_low"], h["layer_high"], h["across"], p, 1 - r)
        return low_rim, high_rim, side_rim, pair_rim

    def rim(h):
        return h["low"][1:], h["high"][:1], h["side"][0], h["pair"]

    def stepped(p, before, coefficient, lap, lap_before):
        change = p - before
        driving = (
            coefficient * lap + viscous * (lap - lap_before) + 2.0 * nonlinear * change * change
        )
        return 2.0 * p - before + (1.0 + 2.0 * nonlinear * p) * driving

    steps = STEPS

    def record(n, p):
        chosen = dot(p.reshape(first * second, third).astype(jnp.bfloat16), at_lane, (1, 0))
        picked = jnp.sum(chosen * at_row, axis=0, keepdims=True)
        for i in range(tiles):
            loads_out[i, n : n + 1, :] = picked[:, i * LANES : (i + 1) * LANES]

    coef_rim = None
    lap_before = None
    for n in range(0, steps, 2):
        ks = (n, n + 1)
        receive(ks + ((4,) if n == 0 else ()))
        now, old = arrived(n), arrived(n + 1)
        if n == 0:
            coef_rim = (low[4][1:], high[4][:1], side_in[4][0], pair_in[4])
            lap_before = lap_own(p_before, old)
        lap = lap_own(p_now, now)
        p_next = stepped(p_now, p_before, courant, lap, lap_before)
        if n + 2 < steps:
            field[1] = p_next
            stage(n + 3, p_next)
            send((n + 3,))
        rims = [
            stepped(*parts)
            for parts in zip(rim(now), rim(old), coef_rim, lap_rim(p_now, now), lap_rim(p_before, old))
        ]
        low_next = jnp.where(has_below, rims[0], 0.0)
        high_next = jnp.where(has_above, rims[1], 0.0)
        lap_next = lap_block(p_next, low_next, high_next, rims[2], rims[3], r)
        p_after = stepped(p_next, p_now, courant, lap_next, lap)
        if n + 2 < steps:
            field[0] = p_after
            stage(n + 2, p_after)
            send((n + 2,))
        else:
            final_ref[...] = p_after
            prior_ref[...] = p_next
        record(n, p_next)
        record(n + 1, p_after)
        p_before, p_now, lap_before = p_next, p_after, lap_next

    def tile_copy(source, target, sems, i):
        to = lax.rem(t + i, tiles)
        return remote(source.at[to], target.at[t], sems, i, {"tile": to})

    loads_copies = [
        tile_copy(loads_out, loads_in, (loads_send, loads_recv), i) for i in range(1, tiles)
    ]
    for copy in loads_copies[::-1]:
        copy.start()
    loads_in[t] = loads_out[t]
    area = area_ref[...].reshape(1, slots)
    lane_row = lax.broadcasted_iota(jnp.int32, (1, LANES), 1)
    areas = []
    for i in range(tiles):
        moved = pltpu.roll(area, (slots - i * bucket) % slots, 1) if i else area
        areas.append(jnp.where(lane_row < bucket, moved[:, :LANES], 0.0))
    for copy in mode_copies:
        copy.wait()
    for copy in loads_copies:
        copy.wait_recv()
    for i in range(tiles):
        weighted[:steps, i * LANES : (i + 1) * LANES] = loads_in[i] * areas[i]
    forces = dot(weighted[...].astype(jnp.bfloat16), modes[...], (1, 0))
    devices = len(partners) + 1
    for i in range(devices):
        force_out[i] = forces[:steps, i * share : (i + 1) * share]

    force_copies = [
        remote(
            force_out.at[linear(place(offset))],
            force_in.at[i],
            (force_send, force_recv),
            i,
            ident(place(offset)),
        )
        for i, offset in enumerate(partners)
    ]
    for copy in force_copies[::-1]:
        copy.start()
    begin = pl.multiple_of(me * share, LANES)
    frequency = frequency_ref[:, pl.ds(begin, share)]
    damping = damping_ref[:, pl.ds(begin, share)]
    started = start_ref[:, pl.ds(begin, share)]
    displace, velocity = started[0:1], started[1:2]
    total = force_out[me]
    for i, copy in enumerate(force_copies):
        copy.wait_recv()
        total = total + force_in[i]
    for n in range(steps):
        accel = (
            total[n : n + 1]
            - 2.0 * damping * frequency * velocity
            - frequency * frequency * displace
        )
        velocity = velocity + accel
        displace = displace + velocity
        accel_out[n : n + 1, :] = accel.astype(jnp.bfloat16).astype(jnp.float32)
    accel_copies = [
        remote(accel_out, accel_in.at[me], (accel_send, accel_recv), i, ident(place(offset)))
        for i, offset in enumerate(partners)
    ]
    for copy in accel_copies[::-1]:
        copy.start()
    state_ref[0:1, :] = displace
    state_ref[1:2, :] = velocity
    accel_in[me] = accel_out[...]
    for copy in accel_copies:
        copy.wait_recv()
    accels = jnp.concatenate([accel_in[i] for i in range(devices)], axis=1)
    node = dot(accels.astype(jnp.bfloat16), modes[...], (1, 1))
    node = node.astype(jnp.bfloat16).astype(jnp.float32)
    for i in range(tiles):
        back_out[i] = node[:, i * LANES : (i + 1) * LANES]
    back_copies = [
        tile_copy(back_out, back_in, (back_send, back_recv), i) for i in range(1, tiles)
    ]
    for copy in back_copies[::-1]:
        copy.start()
    back_in[t] = back_out[t]
    sent((0, 1, 4, 2, 3))
    for copy in loads_copies + force_copies + accel_copies:
        copy.wait_send()
    for copy in back_copies:
        copy.wait_recv()
    returned = jnp.concatenate([back_in[i] for i in range(tiles)], axis=1)
    surface = dot(returned.astype(jnp.bfloat16), route, (1, 0))
    surface_ref[...] = surface.astype(jnp.bfloat16)
    for copy in back_copies:
        copy.wait_send()


def place_kernel(*refs):
    sources, targets, sems = refs[:4], refs[4:8], refs[8]
    copies = [
        pltpu.make_async_copy(source, target, sems.at[i])
        for i, (source, target) in enumerate(zip(sources, targets))
    ]
    for copy in copies:
        copy.start()
    for copy in copies:
        copy.wait()


def fused_body(
    pressure,
    previous_pressure,
    courant_square,
    node_area,
    mode_shapes,
    frequency,
    damping_ratio,
    modal_start,
    slot_cell,
    slot_owner,
    surface_count,
):
    tiles = lax.axis_size("tile")
    devices = tiles * lax.axis_size("sub") * lax.axis_size("rep")
    first, second, third = pressure.shape
    slots = slot_cell.shape[-1]
    modes = mode_shapes.shape[1]
    share = modes // devices
    f32 = jnp.float32
    levels = STEPS + 1
    vmem = pl.BlockSpec(memory_space=pltpu.VMEM)
    dma = pltpu.SemaphoreType.DMA
    shapes = (
        jax.ShapeDtypeStruct(pressure.shape, f32),
        jax.ShapeDtypeStruct(pressure.shape, f32),
        jax.ShapeDtypeStruct((STEPS, slots), jnp.bfloat16),
        jax.ShapeDtypeStruct((2, share), f32),
    )
    outputs = pl.pallas_call(
        functools.partial(window_kernel, tiles),
        out_shape=tuple(pltpu.VMEM(shape.shape, shape.dtype) for shape in shapes),
        in_specs=[pl.BlockSpec(memory_space=pl.ANY)] * 11,
        out_specs=(vmem,) * 4,
        scratch_shapes=[
            pltpu.VMEM(pressure.shape, f32),
            pltpu.VMEM(pressure.shape, f32),
            pltpu.VMEM(pressure.shape, f32),
            pltpu.VMEM(node_area.shape, f32),
            pltpu.VMEM((1, modes), f32),
            pltpu.VMEM((1, modes), f32),
            pltpu.VMEM((2, modes), f32),
            pltpu.VMEM((1, slots), jnp.int32),
            pltpu.VMEM((1, slots), jnp.int32),
            pltpu.VMEM((1, 1, 1), jnp.int32),
            pltpu.VMEM((tiles * LANES, modes), mode_shapes.dtype),
            pltpu.VMEM((2, first, second, third), f32),
            pltpu.VMEM((levels, 2, first, third), f32),
            pltpu.VMEM((levels, 2, 1, third), f32),
            pltpu.VMEM((levels, 2, second, third), f32),
            pltpu.VMEM((levels, 2, second, third), f32),
            pltpu.VMEM((levels, 2, first, third), f32),
            pltpu.VMEM((levels, first, second, third), f32),
            pltpu.VMEM((levels, 2, 1, third), f32),
            pltpu.VMEM((levels, 2, second, third), f32),
            pltpu.VMEM((levels, first, third), f32),
            pltpu.VMEM((tiles, STEPS, LANES), f32),
            pltpu.VMEM((tiles, STEPS, LANES), f32),
            pltpu.VMEM((8, tiles * LANES), f32),
            pltpu.VMEM((devices, STEPS, share), f32),
            pltpu.VMEM((devices, STEPS, share), f32),
            pltpu.VMEM((STEPS, share), f32),
            pltpu.VMEM((devices, STEPS, share), f32),
            pltpu.VMEM((tiles, STEPS, LANES), f32),
            pltpu.VMEM((tiles, STEPS, LANES), f32),
            dma((tiles,)),
            dma((levels, 9)),
            dma((levels, 9)),
            dma((tiles,)),
            dma((tiles,)),
            dma((devices,)),
            dma((devices,)),
            dma((devices,)),
            dma((devices,)),
            dma((tiles,)),
            dma((tiles,)),
            dma((10,)),
        ],
        compiler_params=pltpu.CompilerParams(collective_id=0, has_side_effects=True),
        name="window",
    )(
        pressure,
        previous_pressure,
        courant_square,
        node_area,
        mode_shapes,
        frequency.reshape(1, modes),
        damping_ratio.reshape(1, modes),
        modal_start,
        slot_cell.reshape(1, slots),
        slot_owner.reshape(1, slots),
        surface_count,
    )
    final_field, prior_field, surface, state = pl.pallas_call(
        place_kernel,
        out_shape=shapes,
        in_specs=[vmem] * 4,
        out_specs=(pl.BlockSpec(memory_space=pl.ANY),) * 4,
        scratch_shapes=[dma((4,))],
        name="placed",
    )(*(pltpu.with_memory_space_constraint(x, pltpu.VMEM) for x in outputs))
    return (final_field, prior_field, surface.reshape(1, 1, 1, STEPS, slots), state)


def pick_body(
    pressure,
    previous_pressure,
    courant_square,
    node_area,
    mode_shapes,
    frequency,
    damping_ratio,
    modal_start,
    slot_cell,
    slot_owner,
    surface_count,
):
    tiles, subs, reps = (lax.axis_size(axis) for axis in ("tile", "sub", "rep"))
    bucket = slot_cell.shape[-1] // tiles
    modes = mode_shapes.shape[1]
    fits = (
        subs == 2
        and reps == 2
        and tiles > 1
        and pressure.shape[2] == LANES
        and pressure.shape[1] % 8 == 0
        and pressure.shape[0] % 8 == 0
        and max(pressure.shape[0] * pressure.shape[1], LANES) <= 256
        and bucket <= LANES
        and bucket % 16 == 0
        and slot_cell.shape[-1] % LANES == 0
        and modes % (tiles * subs * reps * LANES) == 0
    )
    return (fused_body if fits else body)(
        pressure,
        previous_pressure,
        courant_square,
        node_area,
        mode_shapes,
        frequency,
        damping_ratio,
        modal_start,
        slot_cell,
        slot_owner,
        surface_count,
    )


def solution(mesh):
    in_specs = (
        P(("groups", "tile"), "sub", "rep"),
        P(("groups", "tile"), "sub", "rep"),
        P(("groups", "tile"), "sub", "rep"),
        P(("groups", "tile", "sub", "rep")),
        P(("groups", "tile", "sub", "rep"), None),
        P("groups"),
        P("groups"),
        P(None, "groups"),
        P(("groups", "tile"), "sub", "rep", None),
        P(("groups", "tile"), "sub", "rep", None, None),
        P(("groups", "sub"), "rep", "tile"),
    )
    out_specs = (
        P(("groups", "tile"), "sub", "rep"),
        P(("groups", "tile"), "sub", "rep"),
        P(("groups", "tile"), "sub", "rep", None, None),
        P(None, ("groups", "tile", "sub", "rep")),
    )
    return jax.shard_map(
        pick_body, mesh=mesh, in_specs=in_specs, out_specs=out_specs, check_vma=False)
```

```python
import functools

import jax
import jax.numpy as jnp
from jax import lax
from jax.experimental import pallas as pl
from jax.experimental.pallas import tpu as pltpu
from jax.sharding import PartitionSpec as P

STEPS = 4
HALO = 4


nonlinear = 0.03
viscous = 0.02


def extended(shard, sides, width):
    for axis, dim in sides:
        count, length = (lax.axis_size(axis), shard.shape[dim])
        up = [(i, (i + 1) % count) for i in range(count - 1)]
        down = [(j, i) for i, j in up]
        last = lax.slice_in_dim(shard, length - width, length, axis=dim)
        first = lax.slice_in_dim(shard, 0, width, axis=dim)
        before = lax.ppermute(last, axis, up)
        after = lax.ppermute(first, axis, down)
        shard = jnp.concatenate([before, shard, after], axis=dim)
    return shard


def laplace(padded):
    middle = padded[1:-1, 1:-1, 1:-1]
    summed = padded[2:, 1:-1, 1:-1] + padded[:-2, 1:-1, 1:-1]
    summed = summed + padded[1:-1, 2:, 1:-1] + padded[1:-1, :-2, 1:-1]
    summed = summed + padded[1:-1, 1:-1, 2:] + padded[1:-1, 1:-1, :-2]
    return summed - 6.0 * middle


def advance(wide_now, wide_before, coefficient):
    current = wide_now[1:-1, 1:-1, 1:-1]
    before = wide_before[1:-1, 1:-1, 1:-1]
    change = current - before
    driving = (
        coefficient * laplace(wide_now)
        + viscous * laplace(wide_now - wide_before)
        + 2.0 * nonlinear * change * change
    )
    return 2.0 * current - before + (1.0 + 2.0 * nonlinear * current) * driving


def routing(owners, live_count, tile_total):
    slot_total = owners.shape[0]
    bucket = slot_total // tile_total
    position = jnp.arange(slot_total, dtype=jnp.int32)
    is_live = position < live_count
    member = (
        (owners[:, None] == jnp.arange(tile_total, dtype=jnp.int32)[None, :]) & is_live[:, None]
    ).astype(jnp.float32)
    earlier = (position[None, :] < position[:, None]).astype(jnp.float32)
    before = jnp.dot(earlier, member, precision=lax.Precision.HIGHEST)
    bucket_rank = jnp.sum(before * member, axis=1).astype(jnp.int32)
    target = owners * bucket + bucket_rank
    return ((target[:, None] == position[None, :]) & is_live[:, None]).astype(jnp.bfloat16)


def oscillate(forces, frequency, damping_ratio, start_state):

    def advance_mode(carried, force_row):
        displace, velocity = carried
        acceleration = (
            force_row
            - 2.0 * damping_ratio * frequency * velocity
            - frequency * frequency * displace
        )
        velocity = velocity + acceleration
        displace = displace + velocity
        return ((displace, velocity), acceleration)

    (displace, velocity), modal_accel = lax.scan(
        advance_mode, (start_state[0], start_state[1]), forces
    )
    return (modal_accel, jnp.stack([displace, velocity]))


def trim_rim(array, depth):
    return array[
        depth : array.shape[0] - depth,
        depth : array.shape[1] - depth,
        depth : array.shape[2] - depth,
    ]


def inside_range(offset, length, axis_devices, margin):
    position = offset * length - margin + jnp.arange(length + 2 * margin, dtype=jnp.int32)
    return ((position >= 0) & (position < axis_devices * length)).astype(jnp.float32)


def body(
    pressure,
    previous_pressure,
    courant_square,
    node_area,
    mode_shapes,
    frequency,
    damping_ratio,
    modal_start,
    slot_cell,
    slot_owner,
    surface_count,
):
    tile_total = lax.axis_size("tile")
    extent_first, extent_second, extent_third = pressure.shape
    slot_total = slot_cell.shape[-1]
    bucket = slot_total // tile_total
    routing_matrix = routing(slot_owner.reshape(slot_total), surface_count.reshape(()), tile_total)
    cell_index = slot_cell.reshape(slot_total)
    fields = jnp.stack([pressure, previous_pressure])
    margin = HALO
    coef_wide = extended(courant_square, (("tile", 0), ("sub", 1), ("rep", 2)), margin)
    inside_first = inside_range(lax.axis_index("tile"), extent_first, lax.axis_size("tile"), margin)
    inside_second = inside_range(lax.axis_index("sub"), extent_second, lax.axis_size("sub"), margin)
    inside_third = inside_range(lax.axis_index("rep"), extent_third, lax.axis_size("rep"), margin)
    inside = (
        inside_first[:, None, None] * inside_second[None, :, None] * inside_third[None, None, :]
    )

    def deep_block(carried, unused):
        padded = extended(carried, (("tile", 1), ("sub", 2), ("rep", 3)), margin)
        recorded = []
        for layer_index in range(margin):
            edge_depth = layer_index + 1
            updated = advance(padded[0], padded[1], trim_rim(coef_wide, edge_depth)) * trim_rim(
                inside, edge_depth
            )
            interior = trim_rim(updated, margin - edge_depth)
            recorded.append(jnp.take(interior.reshape(-1), cell_index).astype(jnp.bfloat16))
            padded = jnp.stack([updated, trim_rim(padded[0], 1)])
        return (padded, jnp.stack(recorded))

    fields, history = lax.scan(deep_block, fields, None, length=STEPS // margin)
    history = history.reshape(STEPS, slot_total)
    final_field = fields[0]
    prior_field = fields[1]
    bucketed = jnp.dot(history, routing_matrix, preferred_element_type=jnp.float32).astype(
        jnp.bfloat16
    )
    bucketed = bucketed.reshape(STEPS, tile_total, bucket)
    arrived = lax.all_to_all(bucketed, "tile", split_axis=1, concat_axis=1, tiled=True)
    arrived_flat = arrived.reshape(arrived.shape[0], slot_total)
    weighted = (arrived_flat * node_area).astype(jnp.bfloat16)
    partial_forces = jnp.dot(weighted, mode_shapes, preferred_element_type=jnp.float32)
    device_total = lax.axis_size("tile") * lax.axis_size("sub") * lax.axis_size("rep")
    mode_count = mode_shapes.shape[1]
    mode_share = mode_count // device_total
    first_mode = lax.axis_index(("tile", "sub", "rep")) * mode_share
    forces = lax.psum_scatter(
        partial_forces, ("tile", "sub", "rep"), scatter_dimension=1, tiled=True
    )
    local_frequency = lax.dynamic_slice_in_dim(frequency, first_mode, mode_share, 0)
    local_damping = lax.dynamic_slice_in_dim(damping_ratio, first_mode, mode_share, 0)
    local_start = lax.dynamic_slice_in_dim(modal_start, first_mode, mode_share, 1)
    modal_accel, modal_state = oscillate(forces, local_frequency, local_damping, local_start)
    modal_rounded = modal_accel.astype(jnp.bfloat16)
    node_accel = lax.dot_general(
        lax.all_gather(modal_rounded, ("tile", "sub", "rep"), axis=1, tiled=True),
        mode_shapes,
        (((1,), (1,)), ((), ())),
        preferred_element_type=jnp.float32,
    )
    outgoing = node_accel.astype(jnp.bfloat16).reshape(STEPS, tile_total, bucket)
    returned = lax.all_to_all(outgoing, "tile", split_axis=1, concat_axis=1, tiled=True)
    surface = lax.dot_general(
        returned.reshape(STEPS, slot_total),
        routing_matrix,
        (((1,), (1,)), ((), ())),
        preferred_element_type=jnp.float32,
    )
    surface_accel = surface.astype(jnp.bfloat16).reshape(1, 1, 1, STEPS, slot_total)
    return (final_field, prior_field, surface_accel, modal_state)

LANES = 128
MESH = pl.DeviceIdType.MESH


def other_devices(tiles, subs, reps):
    return [
        (i, j, k)
        for i in range(tiles)
        for j in range(subs)
        for k in range(reps)
        if (i, j, k) != (0, 0, 0)
    ]


def dot(a, b, contract):
    return lax.dot_general(a, b, ((contract[:1], contract[1:]), ((), ())), preferred_element_type=jnp.float32)


def window_kernel(
    tiles,
    pressure_hbm,
    previous_hbm,
    courant_hbm,
    area_hbm,
    modes_hbm,
    frequency_hbm,
    damping_hbm,
    start_hbm,
    cell_hbm,
    owner_hbm,
    count_hbm,
    final_ref,
    prior_ref,
    surface_ref,
    state_ref,
    pressure_ref,
    previous_ref,
    courant_ref,
    area_ref,
    frequency_ref,
    damping_ref,
    start_ref,
    cell_ref,
    owner_ref,
    count_ref,
    modes,
    field,
    side_out,
    corner_out,
    low,
    high,
    side_in,
    pair_in,
    corner_in,
    layer_in,
    across_in,
    loads_out,
    loads_in,
    weighted,
    force_out,
    force_in,
    accel_out,
    accel_in,
    back_out,
    back_in,
    modes_sem,
    halo_send,
    halo_recv,
    loads_send,
    loads_recv,
    force_send,
    force_recv,
    accel_send,
    accel_recv,
    back_send,
    back_recv,
    input_sem,
):
    t, s, r = lax.axis_index("tile"), lax.axis_index("sub"), lax.axis_index("rep")
    first, second, third = pressure_ref.shape
    slots = cell_ref.shape[1]
    bucket = slots // tiles
    padded_rows = tiles * LANES
    partners = other_devices(tiles, 2, 2)
    share = state_ref.shape[1]
    me = (t * 2 + s) * 2 + r

    def place(offset):
        i, j, k = offset
        return (lax.rem(t + i, tiles), lax.rem(s + j, 2), lax.rem(r + k, 2))

    def ident(where):
        return {"tile": where[0], "sub": where[1], "rep": where[2]}

    def linear(where):
        return (where[0] * 2 + where[1]) * 2 + where[2]

    barrier = pltpu.get_barrier_semaphore()
    up = {"tile": jnp.minimum(t + 1, tiles - 1)}
    down = {"tile": jnp.maximum(t - 1, 0)}
    beside_me, pair = {"sub": 1 - s}, {"rep": 1 - r}
    in_tile = ({}, beside_me, pair, beside_me | pair)

    def greet(devices):
        for where in devices:
            pl.semaphore_signal(barrier, inc=1, device_id=where, device_id_type=MESH)

    @pl.when(t < tiles - 1)
    def _():
        greet([up | where for where in in_tile])

    @pl.when(t > 0)
    def _():
        greet([down | where for where in in_tile])

    greet(in_tile[1:])

    mode_copies = [
        pltpu.make_async_copy(
            modes_hbm.at[pl.ds(i * bucket, bucket)],
            modes.at[pl.ds(i * LANES, bucket)],
            modes_sem.at[i],
        )
        for i in range(tiles)
    ]
    inputs = [
        (pressure_hbm, pressure_ref),
        (previous_hbm, previous_ref),
        (courant_hbm, courant_ref),
        (area_hbm, area_ref),
        (frequency_hbm, frequency_ref),
        (damping_hbm, damping_ref),
        (start_hbm, start_ref),
        (cell_hbm, cell_ref),
        (owner_hbm, owner_ref),
        (count_hbm, count_ref),
    ]
    input_copies = [
        pltpu.make_async_copy(source, held, input_sem.at[i])
        for i, (source, held) in enumerate(inputs)
    ]
    for copy in input_copies:
        copy.start()
    for copy in mode_copies:
        copy.start()

    def near(value):
        return jnp.where(s == 0, value[:, second - 1, :], value[:, 0, :])

    def next_near(value):
        return jnp.where(s == 0, value[:, second - 2, :], value[:, 1, :])

    def stage(k, value):
        rows = near(value)
        side_out[k, 0] = rows
        side_out[k, 1] = next_near(value)
        corner_out[k, 0] = rows[:1]
        corner_out[k, 1] = rows[first - 1 :]

    for copy in input_copies:
        copy.wait()
    p_now, p_before = pressure_ref[...], previous_ref[...]
    courant = courant_ref[...]
    stage(0, p_now)
    stage(1, p_before)
    stage(4, courant)

    def level(k):
        return (pressure_ref, previous_ref, field.at[0], field.at[1], courant_ref)[k]

    def remote(source, target, sems, index, where):
        return pltpu.make_async_remote_copy(
            src_ref=source,
            dst_ref=target,
            send_sem=sems[0].at[index],
            recv_sem=sems[1].at[index],
            device_id=where,
            device_id_type=MESH,
        )

    def piece(k, m):
        source, target, where = (
            (level(k).at[pl.ds(first - 2, 2)], low.at[k], up),
            (level(k).at[pl.ds(0, 2)], high.at[k], down),
            (side_out.at[k], side_in.at[k], beside_me),
            (level(k), pair_in.at[k], pair),
            (corner_out.at[k, 1], corner_in.at[k, 0], up | beside_me),
            (corner_out.at[k, 0], corner_in.at[k, 1], down | beside_me),
            (level(k).at[first - 1], layer_in.at[k, 0], up | pair),
            (level(k).at[0], layer_in.at[k, 1], down | pair),
            (side_out.at[k, 0], across_in.at[k], beside_me | pair),
        )[m]
        return remote(source, target, (halo_send, halo_recv), (k, m), where)

    def pieces(k):
        return (0, 1, 2, 3) if k == 4 else (0, 1, 6, 7, 4, 5, 8, 2, 3)

    def each(ks, upward, act):
        todo = [(k, m) for k in ks for m in pieces(k)]

        def run(chosen):
            for k, m in todo:
                if m in chosen:
                    act(piece(k, m))

        @pl.when(t < tiles - 1)
        def _():
            run((0, 4, 6) if upward else (1, 5, 7))

        @pl.when(t > 0)
        def _():
            run((1, 5, 7) if upward else (0, 4, 6))

        run((2, 3, 8))

    def send(ks):
        each(ks, True, lambda copy: copy.start())

    def receive(ks):
        each(ks, False, lambda copy: copy.wait_recv())

    def sent(ks):
        each(ks, True, lambda copy: copy.wait_send())

    greeted = 4 * (jnp.minimum(t, 1) + jnp.minimum(tiles - 1 - t, 1)) + 3
    pl.semaphore_wait(barrier, greeted)
    send((0, 1, 4))

    for i in range(tiles):
        if bucket < LANES:
            modes[i * LANES + bucket : (i + 1) * LANES, :] = jnp.zeros(
                (LANES - bucket, modes.shape[1]), modes.dtype
            )
    weighted[...] = jnp.zeros_like(weighted)
    owner = owner_ref[...]
    cell = cell_ref[...]
    lane = lax.broadcasted_iota(jnp.int32, (1, slots), 1)
    live = lane < count_ref[0]
    owner_live = jnp.where(live, owner, -1)
    height = -(-tiles // 8) * 8
    member = (
        lax.broadcasted_iota(jnp.int32, (height, slots), 0) == owner_live
    ).astype(jnp.float32)
    earlier = (
        lax.broadcasted_iota(jnp.int32, (slots, slots), 0)
        < lax.broadcasted_iota(jnp.int32, (slots, slots), 1)
    ).astype(jnp.float32).astype(jnp.bfloat16)
    before = dot(member.astype(jnp.bfloat16), earlier, (1, 0))
    rank = jnp.sum(before * member, axis=0, keepdims=True).astype(jnp.int32)
    target = jnp.where(live, owner * LANES + rank, -1)
    route = (
        (lax.broadcasted_iota(jnp.int32, (padded_rows, slots), 0) == target)
        .astype(jnp.float32)
        .astype(jnp.bfloat16)
    )
    row_of = cell // third
    lane_of = cell - row_of * third
    pick_row = (
        (lax.broadcasted_iota(jnp.int32, (first * second, slots), 0) == row_of)
        .astype(jnp.float32)
        .astype(jnp.bfloat16)
    )
    pick_lane = (
        (lax.broadcasted_iota(jnp.int32, (third, slots), 0) == lane_of)
        .astype(jnp.float32)
        .astype(jnp.bfloat16)
    )
    at_row = dot(pick_row, route, (1, 1))
    at_lane = dot(pick_lane, route, (1, 1)).astype(jnp.bfloat16)

    at_second = lax.broadcasted_iota(jnp.int32, (1, second, third), 1)
    at_third = lax.broadcasted_iota(jnp.int32, (1, 1, third), 2)
    edge_row = jnp.where(s == 0, second - 1, 0)

    def along_lanes(p, q, half, lanes):
        axis = p.ndim - 1
        total = jnp.where(lanes == 0, 0.0, pltpu.roll(p, 1, axis))
        total = total + jnp.where(lanes == third - 1, 0.0, pltpu.roll(p, third - 1, axis))
        edge = jnp.where(half == 0, third - 1, 0)
        shifted = jnp.where(half == 0, pltpu.roll(q, third - 1, axis), pltpu.roll(q, 1, axis))
        return total + jnp.where(lanes == edge, shifted, 0.0)

    def lap_block(p, below, above, beside, q, half):
        total = along_lanes(p, q, half, at_third) - 6.0 * p
        if p.shape[0] > 1:
            below = jnp.concatenate([below, p[:-1]], axis=0)
            above = jnp.concatenate([p[1:], above], axis=0)
        total = total + below + above
        total = total + jnp.where(at_second == 0, 0.0, pltpu.roll(p, 1, 1))
        total = total + jnp.where(at_second == second - 1, 0.0, pltpu.roll(p, second - 1, 1))
        return total + jnp.where(at_second == edge_row, beside[:, None, :], 0.0)

    at_layer = lax.broadcasted_iota(jnp.int32, (first, third), 0)
    at_lane_side = lax.broadcasted_iota(jnp.int32, (1, third), 1)

    def lap_side(g, inward, outward, below, above, q):
        total = along_lanes(g, q, r, at_lane_side) - 6.0 * g
        total = total + inward + outward
        total = total + jnp.where(at_layer == 0, below, pltpu.roll(g, 1, 0))
        return total + jnp.where(at_layer == first - 1, above, pltpu.roll(g, first - 1, 0))

    has_below, has_above = t > 0, t < tiles - 1

    def arrived(k):
        return dict(
            low=jnp.where(has_below, low[k], 0.0),
            high=jnp.where(has_above, high[k], 0.0),
            side=side_in[k],
            pair=pair_in[k],
            corner_low=jnp.where(has_below, corner_in[k, 0], 0.0),
            corner_high=jnp.where(has_above, corner_in[k, 1], 0.0),
            layer_low=jnp.where(has_below, layer_in[k, 0], 0.0)[None],
            layer_high=jnp.where(has_above, layer_in[k, 1], 0.0)[None],
            across=across_in[k],
        )

    def lap_own(p, h):
        return lap_block(p, h["low"][1:], h["high"][:1], h["side"][0], h["pair"], r)

    def lap_rim(p, h):
        low_rim = lap_block(
            h["low"][1:], h["low"][:1], p[:1], h["corner_low"], h["layer_low"], r
        )
        high_rim = lap_block(
            h["high"][:1], p[first - 1 :], h["high"][1:], h["corner_high"], h["layer_high"], r
        )
        side_rim = lap_side(
            h["side"][0], near(p), h["side"][1], h["corner_low"], h["corner_high"], h["across"]
        )
        pair_rim = lap_block(h["pair"], h["layer_low"], h["layer_high"], h["across"], p, 1 - r)
        return low_rim, high_rim, side_rim, pair_rim

    def rim(h):
        return h["low"][1:], h["high"][:1], h["side"][0], h["pair"]

    def stepped(p, before, coefficient, lap, lap_before):
        change = p - before
        driving = (
            coefficient * lap + viscous * (lap - lap_before) + 2.0 * nonlinear * change * change
        )
        return 2.0 * p - before + (1.0 + 2.0 * nonlinear * p) * driving

    steps = STEPS

    def record(n, p):
        chosen = dot(p.reshape(first * second, third).astype(jnp.bfloat16), at_lane, (1, 0))
        picked = jnp.sum(chosen * at_row, axis=0, keepdims=True)
        for i in range(tiles):
            loads_out[i, n : n + 1, :] = picked[:, i * LANES : (i + 1) * LANES]

    coef_rim = None
    lap_before = None
    for n in range(0, steps, 2):
        ks = (n, n + 1)
        receive(ks + ((4,) if n == 0 else ()))
        now, old = arrived(n), arrived(n + 1)
        if n == 0:
            coef_rim = (low[4][1:], high[4][:1], side_in[4][0], pair_in[4])
            lap_before = lap_own(p_before, old)
        lap = lap_own(p_now, now)
        p_next = stepped(p_now, p_before, courant, lap, lap_before)
        if n + 2 < steps:
            field[1] = p_next
            stage(n + 3, p_next)
            send((n + 3,))
        rims = [
            stepped(*parts)
            for parts in zip(rim(now), rim(old), coef_rim, lap_rim(p_now, now), lap_rim(p_before, old))
        ]
        low_next = jnp.where(has_below, rims[0], 0.0)
        high_next = jnp.where(has_above, rims[1], 0.0)
        lap_next = lap_block(p_next, low_next, high_next, rims[2], rims[3], r)
        p_after = stepped(p_next, p_now, courant, lap_next, lap)
        if n + 2 < steps:
            field[0] = p_after
            stage(n + 2, p_after)
            send((n + 2,))
        else:
            final_ref[...] = p_after
            prior_ref[...] = p_next
        record(n, p_next)
        record(n + 1, p_after)
        p_before, p_now, lap_before = p_next, p_after, lap_next

    def tile_copy(source, target, sems, i):
        to = lax.rem(t + i, tiles)
        return remote(source.at[to], target.at[t], sems, i, {"tile": to})

    loads_copies = [
        tile_copy(loads_out, loads_in, (loads_send, loads_recv), i) for i in range(1, tiles)
    ]
    for copy in loads_copies[::-1]:
        copy.start()
    loads_in[t] = loads_out[t]
    area = area_ref[...].reshape(1, slots)
    lane_row = lax.broadcasted_iota(jnp.int32, (1, LANES), 1)
    areas = []
    for i in range(tiles):
        moved = pltpu.roll(area, (slots - i * bucket) % slots, 1) if i else area
        areas.append(jnp.where(lane_row < bucket, moved[:, :LANES], 0.0))
    for copy in mode_copies:
        copy.wait()
    for copy in loads_copies:
        copy.wait_recv()
    for i in range(tiles):
        weighted[:steps, i * LANES : (i + 1) * LANES] = loads_in[i] * areas[i]
    forces = dot(weighted[...].astype(jnp.bfloat16), modes[...], (1, 0))
    devices = len(partners) + 1
    for i in range(devices):
        force_out[i] = forces[:steps, i * share : (i + 1) * share]

    force_copies = [
        remote(
            force_out.at[linear(place(offset))],
            force_in.at[i],
            (force_send, force_recv),
            i,
            ident(place(offset)),
        )
        for i, offset in enumerate(partners)
    ]
    for copy in force_copies[::-1]:
        copy.start()
    begin = pl.multiple_of(me * share, LANES)
    frequency = frequency_ref[:, pl.ds(begin, share)]
    damping = damping_ref[:, pl.ds(begin, share)]
    started = start_ref[:, pl.ds(begin, share)]
    displace, velocity = started[0:1], started[1:2]
    total = force_out[me]
    for i, copy in enumerate(force_copies):
        copy.wait_recv()
        total = total + force_in[i]
    for n in range(steps):
        accel = (
            total[n : n + 1]
            - 2.0 * damping * frequency * velocity
            - frequency * frequency * displace
        )
        velocity = velocity + accel
        displace = displace + velocity
        accel_out[n : n + 1, :] = accel.astype(jnp.bfloat16).astype(jnp.float32)
    accel_copies = [
        remote(accel_out, accel_in.at[me], (accel_send, accel_recv), i, ident(place(offset)))
        for i, offset in enumerate(partners)
    ]
    for copy in accel_copies[::-1]:
        copy.start()
    state_ref[0:1, :] = displace
    state_ref[1:2, :] = velocity
    accel_in[me] = accel_out[...]
    for copy in accel_copies:
        copy.wait_recv()
    accels = jnp.concatenate([accel_in[i] for i in range(devices)], axis=1)
    node = dot(accels.astype(jnp.bfloat16), modes[...], (1, 1))
    node = node.astype(jnp.bfloat16).astype(jnp.float32)
    for i in range(tiles):
        back_out[i] = node[:, i * LANES : (i + 1) * LANES]
    back_copies = [
        tile_copy(back_out, back_in, (back_send, back_recv), i) for i in range(1, tiles)
    ]
    for copy in back_copies[::-1]:
        copy.start()
    back_in[t] = back_out[t]
    sent((0, 1, 4, 2, 3))
    for copy in loads_copies + force_copies + accel_copies:
        copy.wait_send()
    for copy in back_copies:
        copy.wait_recv()
    returned = jnp.concatenate([back_in[i] for i in range(tiles)], axis=1)
    surface = dot(returned.astype(jnp.bfloat16), route, (1, 0))
    surface_ref[...] = surface.astype(jnp.bfloat16)
    for copy in back_copies:
        copy.wait_send()


def place_kernel(*refs):
    sources, targets, sems = refs[:4], refs[4:8], refs[8]
    copies = [
        pltpu.make_async_copy(source, target, sems.at[i])
        for i, (source, target) in enumerate(zip(sources, targets))
    ]
    for copy in copies:
        copy.start()
    for copy in copies:
        copy.wait()


def fused_body(
    pressure,
    previous_pressure,
    courant_square,
    node_area,
    mode_shapes,
    frequency,
    damping_ratio,
    modal_start,
    slot_cell,
    slot_owner,
    surface_count,
):
    tiles = lax.axis_size("tile")
    devices = tiles * lax.axis_size("sub") * lax.axis_size("rep")
    first, second, third = pressure.shape
    slots = slot_cell.shape[-1]
    modes = mode_shapes.shape[1]
    share = modes // devices
    f32 = jnp.float32
    levels = STEPS + 1
    vmem = pl.BlockSpec(memory_space=pltpu.VMEM)
    dma = pltpu.SemaphoreType.DMA
    shapes = (
        jax.ShapeDtypeStruct(pressure.shape, f32),
        jax.ShapeDtypeStruct(pressure.shape, f32),
        jax.ShapeDtypeStruct((STEPS, slots), jnp.bfloat16),
        jax.ShapeDtypeStruct((2, share), f32),
    )
    outputs = pl.pallas_call(
        functools.partial(window_kernel, tiles),
        out_shape=tuple(pltpu.VMEM(shape.shape, shape.dtype) for shape in shapes),
        in_specs=[pl.BlockSpec(memory_space=pl.ANY)] * 11,
        out_specs=(vmem,) * 4,
        scratch_shapes=[
            pltpu.VMEM(pressure.shape, f32),
            pltpu.VMEM(pressure.shape, f32),
            pltpu.VMEM(pressure.shape, f32),
            pltpu.VMEM(node_area.shape, f32),
            pltpu.VMEM((1, modes), f32),
            pltpu.VMEM((1, modes), f32),
            pltpu.VMEM((2, modes), f32),
            pltpu.VMEM((1, slots), jnp.int32),
            pltpu.VMEM((1, slots), jnp.int32),
            pltpu.VMEM((1, 1, 1), jnp.int32),
            pltpu.VMEM((tiles * LANES, modes), mode_shapes.dtype),
            pltpu.VMEM((2, first, second, third), f32),
            pltpu.VMEM((levels, 2, first, third), f32),
            pltpu.VMEM((levels, 2, 1, third), f32),
            pltpu.VMEM((levels, 2, second, third), f32),
            pltpu.VMEM((levels, 2, second, third), f32),
            pltpu.VMEM((levels, 2, first, third), f32),
            pltpu.VMEM((levels, first, second, third), f32),
            pltpu.VMEM((levels, 2, 1, third), f32),
            pltpu.VMEM((levels, 2, second, third), f32),
            pltpu.VMEM((levels, first, third), f32),
            pltpu.VMEM((tiles, STEPS, LANES), f32),
            pltpu.VMEM((tiles, STEPS, LANES), f32),
            pltpu.VMEM((8, tiles * LANES), f32),
            pltpu.VMEM((devices, STEPS, share), f32),
            pltpu.VMEM((devices, STEPS, share), f32),
            pltpu.VMEM((STEPS, share), f32),
            pltpu.VMEM((devices, STEPS, share), f32),
            pltpu.VMEM((tiles, STEPS, LANES), f32),
            pltpu.VMEM((tiles, STEPS, LANES), f32),
            dma((tiles,)),
            dma((levels, 9)),
            dma((levels, 9)),
            dma((tiles,)),
            dma((tiles,)),
            dma((devices,)),
            dma((devices,)),
            dma((devices,)),
            dma((devices,)),
            dma((tiles,)),
            dma((tiles,)),
            dma((10,)),
        ],
        compiler_params=pltpu.CompilerParams(collective_id=0, has_side_effects=True),
        name="window",
    )(
        pressure,
        previous_pressure,
        courant_square,
        node_area,
        mode_shapes,
        frequency.reshape(1, modes),
        damping_ratio.reshape(1, modes),
        modal_start,
        slot_cell.reshape(1, slots),
        slot_owner.reshape(1, slots),
        surface_count,
    )
    final_field, prior_field, surface, state = pl.pallas_call(
        place_kernel,
        out_shape=shapes,
        in_specs=[vmem] * 4,
        out_specs=(pl.BlockSpec(memory_space=pl.ANY),) * 4,
        scratch_shapes=[dma((4,))],
        name="placed",
    )(*(pltpu.with_memory_space_constraint(x, pltpu.VMEM) for x in outputs))
    return (final_field, prior_field, surface.reshape(1, 1, 1, STEPS, slots), state)


def pick_body(
    pressure,
    previous_pressure,
    courant_square,
    node_area,
    mode_shapes,
    frequency,
    damping_ratio,
    modal_start,
    slot_cell,
    slot_owner,
    surface_count,
):
    tiles, subs, reps = (lax.axis_size(axis) for axis in ("tile", "sub", "rep"))
    bucket = slot_cell.shape[-1] // tiles
    modes = mode_shapes.shape[1]
    fits = (
        subs == 2
        and reps == 2
        and 1 < tiles <= 4
        and pressure.shape[2] == LANES
        and pressure.shape[1] % 8 == 0
        and pressure.shape[0] % 8 == 0
        and max(pressure.shape[0] * pressure.shape[1], LANES) <= 256
        and bucket <= LANES
        and bucket % 16 == 0
        and slot_cell.shape[-1] % LANES == 0
        and modes % (tiles * subs * reps * LANES) == 0
    )
    return (fused_body if fits else body)(
        pressure,
        previous_pressure,
        courant_square,
        node_area,
        mode_shapes,
        frequency,
        damping_ratio,
        modal_start,
        slot_cell,
        slot_owner,
        surface_count,
    )


def solution(mesh):
    in_specs = (
        P(("groups", "tile"), "sub", "rep"),
        P(("groups", "tile"), "sub", "rep"),
        P(("groups", "tile"), "sub", "rep"),
        P(("groups", "tile", "sub", "rep")),
        P(("groups", "tile", "sub", "rep"), None),
        P("groups"),
        P("groups"),
        P(None, "groups"),
        P(("groups", "tile"), "sub", "rep", None),
        P(("groups", "tile"), "sub", "rep", None, None),
        P(("groups", "sub"), "rep", "tile"),
    )
    out_specs = (
        P(("groups", "tile"), "sub", "rep"),
        P(("groups", "tile"), "sub", "rep"),
        P(("groups", "tile"), "sub", "rep", None, None),
        P(None, ("groups", "tile", "sub", "rep")),
    )
    return jax.shard_map(
        pick_body, mesh=mesh, in_specs=in_specs, out_specs=out_specs, check_vma=False)
```
